128 devices in a mesh: row: 32 (over y_hi, x, z), rep: 4 (over y_lo, core).
Axes of the slice: x: 4, y: 4 (y_hi: 2, y_lo: 2; y = y_hi * 2 + y_lo), z: 4, core: 2. Of those that a mesh axis runs over, the one named last changes fastest.
Arguments:
- features: bfloat16 [16384, 256], P('row'), may hold values from -6 to 6
- weight: bfloat16 [256, 256], replicated, may hold values from -0.375 to 0.375
- adj_tiles: bfloat16 [128, 64, 128, 128], P('row', 'rep'), as said below
- block_cols: int32 [128, 64], P('row', 'rep'), may hold values from 0 to 127, as said below
- edge_keep: int32 [128, 64], P('row', 'rep'), may hold values 0 or 1
- drop_key: int32 [2], replicated, may hold values from 0 to 1048575
- cotangent: bfloat16 [16384, 256], P('row'), may hold values from -6 to 6
Outputs:
- hidden: bfloat16 [16384, 256], P('row')
- weight_grad: float32 [256, 256], replicated
- feature_grad: bfloat16 [16384, 256], P(('row', 'rep'))
The draws below stay inside these ranges and needn't reach their ends.
Inputs may be any that keep to these rules, and one draw needn't show every extreme that they name: For slot k of block row i, the group block_cols[i, k] // 4 is congruent to i // 4 - k // 16 modulo 4. `adj_tiles`: entries are zero or positive.
All inputs are finite; a program needn't handle non-finite values. No bound on the sum of `edge_keep` on one device may be relied on, other than what follows from the above.
Results may differ from the reference program's by a relative error of at most 0.022.
Values may be sent and summed in bfloat16 or wider, within the bound.
A program may use at most 64 MiB of HBM per device.

```python
import jax
import jax.numpy as jnp
from jax import lax

BLK = 128
FEAT = 256
BR_DEV = 4
KQ = 16
NB = 128
SLOTS = 64
NODES = 16384
N_ROW = 32
N_REP = 4


def draw_adj_tiles(key, part):
    density_key = jax.random.fold_in(key, 11)
    present_key = jax.random.fold_in(key, 12)
    value_key = jax.random.fold_in(key, 13)
    shape = (NB, SLOTS, BLK, BLK)
    density = jnp.exp(jax.random.uniform(density_key, (NB, 1, BLK, 1), jnp.float32, -1.2, 1.2)) * (20.0 / (SLOTS * BLK))
    present = jax.random.uniform(present_key, shape, jnp.float32) < density
    value = jnp.exp(jax.random.uniform(value_key, shape, jnp.float32, -1.3862944, 0.0))
    return jnp.where(present, value, jnp.zeros(shape, jnp.float32)).astype(jnp.bfloat16)


def draw_block_cols(key, part):
    hop_key = jax.random.fold_in(key, 21)
    within_key = jax.random.fold_in(key, 22)
    block_row = jax.lax.broadcasted_iota(jnp.int32, (NB, SLOTS), 0)
    slot_index = jax.lax.broadcasted_iota(jnp.int32, (NB, SLOTS), 1)
    group_row = block_row // BR_DEV
    replica = slot_index // KQ
    hop_index = jax.random.randint(hop_key, (NB, SLOTS), 0, N_ROW // N_REP, jnp.int32)
    within = jax.random.randint(within_key, (NB, SLOTS), 0, BR_DEV, jnp.int32)
    group_idx = jnp.mod(group_row - replica - N_REP * hop_index, N_ROW)
    return (group_idx * BR_DEV + within).astype(jnp.int32)


def plant(values, rng, low, largest):
    index_at = [jax.random.randint(jax.random.fold_in(rng, axis), (), 0, length) for axis, length in enumerate(values.shape)]
    widest = values.shape.index(max(values.shape))
    neighbour = index_at[:widest] + [(index_at[widest] + 1) % values.shape[widest]] + index_at[widest + 1:]
    return values.at[tuple(index_at)].set(low).at[tuple(neighbour)].set(largest)


def level_of(stream_key, dims, split, smallest, largest):
    gain, own = 1.0, jax.random.fold_in(stream_key, 6)
    for dim, parts in split:
        steps = jnp.exp(jax.random.uniform(jax.random.fold_in(own, dim), (parts,), jnp.float32, smallest / len(split), largest / len(split)))
        gain = gain * jnp.repeat(steps, dims[dim] // parts).reshape([-1 if axis == dim else 1 for axis in range(len(dims))])
    return gain


def noise(rng, dims, deviation, reach, split=(), held_as=jnp.bfloat16):
    values = jax.random.normal(rng, dims, jnp.float32) * deviation
    if len(split) > 0:
        values = level_of(rng, dims, split, -0.22, 0.18) * values
    return jnp.clip(values, min=-reach, max=reach).astype(held_as)


def setup_inputs(seed: int = 0) -> dict:
    seeds = jax.random.split(jax.random.key(seed), 8)
    return {
        "features": noise(seeds[0], (NODES, FEAT), 1.0, 6.0, ((0, 32),)),
        "weight": noise(seeds[1], (FEAT, FEAT), FEAT ** -0.5, 0.375),
        "adj_tiles": draw_adj_tiles(jax.random.fold_in(seeds[7], 71), 0),
        "block_cols": draw_block_cols(jax.random.fold_in(seeds[7], 71), 0),
        "edge_keep": plant((jax.random.randint(seeds[4], (NB, SLOTS), 0, 5) < 4).astype(jnp.int32), jax.random.fold_in(seeds[4], 1), 0, 1),
        "drop_key": jax.random.randint(seeds[5], (2,), 0, 1048576).astype(jnp.int32),
        "cotangent": noise(seeds[6], (NODES, FEAT), 1.0, 6.0, ((0, 32),)),
    }


def keep_mask(node_ids, feat_ids, drop_key):
    mixed_hash = node_ids * 73856093 ^ feat_ids * 19349663 ^ drop_key[0] * 83492791 ^ drop_key[1]
    mixed_hash = mixed_hash ^ lax.shift_right_logical(mixed_hash, jnp.int32(13))
    mixed_hash = mixed_hash * 1274126177
    mixed_hash = mixed_hash ^ lax.shift_right_logical(mixed_hash, jnp.int32(16))
    return mixed_hash & 1023 < 819

def reference(features, weight, adj_tiles, block_cols, edge_keep, drop_key, cotangent):
    node_ids = lax.broadcasted_iota(jnp.int32, (NODES, FEAT), 0)
    feat_ids = lax.broadcasted_iota(jnp.int32, (NODES, FEAT), 1)
    kept_mask = keep_mask(node_ids, feat_ids, drop_key.astype(jnp.int32))
    masked = jnp.where(kept_mask, features, jnp.zeros_like(features))
    gated_tiles = adj_tiles * edge_keep[:, :, None, None].astype(jnp.bfloat16)
    columns = block_cols.astype(jnp.int32)

    def degree_row(carry, pair):
        row_tiles, row_cols = pair
        tiles_wide = row_tiles.astype(jnp.float32)
        col_part = lax.optimization_barrier(jnp.sum(tiles_wide, axis=1))
        row_part = lax.optimization_barrier(jnp.sum(tiles_wide, axis=(0, 2)))
        return (carry.at[row_cols].add(col_part), row_part)
    col_total, row_total = lax.scan(degree_row, jnp.zeros((NB, BLK), jnp.float32), (gated_tiles, columns))
    row_scale = lax.rsqrt(1.0 + row_total)[..., None]
    col_scale = lax.rsqrt(1.0 + col_total)
    scaled = (jnp.dot(masked, weight, preferred_element_type=jnp.float32) * 1.25 * col_scale.reshape(NODES, 1)).astype(jnp.bfloat16)
    blocks = scaled.reshape(NB, BLK, FEAT)

    def aggregate_row(pair):
        row_tiles, row_cols = pair
        gathered = blocks[row_cols]
        return jnp.einsum('kab,kbf->af', row_tiles.astype(jnp.float32), gathered.astype(jnp.float32), precision=lax.Precision.HIGHEST)
    summed = lax.map(aggregate_row, (gated_tiles, columns))
    preact = row_scale * (summed + blocks.astype(jnp.float32))
    sigmoid_val = jax.nn.sigmoid(preact)
    hidden = (preact * sigmoid_val).astype(jnp.bfloat16)
    pre_grad = cotangent.astype(jnp.float32).reshape(NB, BLK, FEAT) * sigmoid_val * (1.0 + preact * (1.0 - sigmoid_val))
    self_term = pre_grad * row_scale
    pushed = self_term.astype(jnp.bfloat16)

    def scatter_row(partial_value, triple):
        row_tiles, row_cols, row_push = triple
        contribution = jnp.einsum('kab,af->kbf', row_tiles.astype(jnp.float32), row_push.astype(jnp.float32), precision=lax.Precision.HIGHEST)
        return (partial_value.at[row_cols].add(contribution), None)
    transposed, _ = lax.scan(scatter_row, jnp.zeros((NB, BLK, FEAT), jnp.float32), (gated_tiles, columns, pushed))
    proj_grad = (col_scale[..., None] * (self_term + transposed)).astype(jnp.bfloat16).reshape(NODES, FEAT)
    weight_grad = jnp.dot(masked.T, proj_grad, preferred_element_type=jnp.float32) * 1.25
    feature_grad = jnp.where(kept_mask, jnp.dot(proj_grad, weight.T, preferred_element_type=jnp.float32) * 1.25, jnp.zeros((NODES, FEAT), jnp.float32)).astype(jnp.bfloat16)
    return (hidden.reshape(NODES, FEAT), weight_grad, feature_grad)
```

```python
import functools

import jax
import jax.numpy as jnp
from jax import lax
from jax.experimental import pallas as pl
from jax.experimental.pallas import tpu as pltpu
from jax.sharding import PartitionSpec as P

MESH = pl.DeviceIdType.MESH
BLK = 128
FEAT = 256
ROWS = 512
F32 = jnp.float32
BF16 = jnp.bfloat16


def keep_mask(node_ids, feat_ids, key0, key1):
    mixed = node_ids * 73856093 ^ feat_ids * 19349663 ^ key0 * 83492791 ^ key1
    mixed = mixed ^ lax.shift_right_logical(mixed, jnp.int32(13))
    mixed = mixed * 1274126177
    mixed = mixed ^ lax.shift_right_logical(mixed, jnp.int32(16))
    return mixed & 1023 < 819


def place(y, x, z, c):
    y, x, z = y % 4, x % 4, z % 4
    return ((y // 2) * 16 + x * 4 + z, (y % 2) * 2 + c)


def build_kernel(idx_ref, keep_ref, tiles_ref, d_ref, col_ref, row_ref):
    i = pl.program_id(0)

    @pl.when(i == 0)
    def _():
        col_ref[...] = jnp.zeros_like(col_ref)

    d_ref[...] = jnp.zeros_like(d_ref)
    row_acc = jnp.zeros((BLK, BLK), F32)
    for k in range(16):
        slot = idx_ref[i, k]
        tile = tiles_ref[0, k].astype(F32) * keep_ref[i, k].astype(F32)
        at = pl.ds(pl.multiple_of(slot * BLK, BLK), BLK)
        d_ref[:, at] = (d_ref[:, at].astype(F32) + tile).astype(BF16)
        col_ref[pl.ds(slot, 1), :] += jnp.sum(tile, axis=0, keepdims=True)
        row_acc = row_acc + tile
    row_ref[pl.ds(i, 1), :] = jnp.sum(row_acc.T, axis=0, keepdims=True)


def build(idx, keep, tiles):
    return pl.pallas_call(
        build_kernel,
        grid_spec=pltpu.PrefetchScalarGridSpec(
            num_scalar_prefetch=2,
            grid=(4,),
            in_specs=[pl.BlockSpec((1, 16, BLK, BLK), lambda i, a, b: (i, 0, 0, 0))],
            out_specs=[
                pl.BlockSpec((BLK, 32 * BLK), lambda i, a, b: (i, 0)),
                pl.BlockSpec((32, BLK), lambda i, a, b: (0, 0)),
                pl.BlockSpec((4, BLK), lambda i, a, b: (0, 0)),
            ],
        ),
        out_shape=[
            jax.ShapeDtypeStruct((ROWS, 32 * BLK), BF16),
            jax.ShapeDtypeStruct((32, BLK), F32),
            jax.ShapeDtypeStruct((4, BLK), F32),
        ],
        name="build",
    )(idx, keep, tiles)


def layer_kernel(
    key_ref, feat_hbm, w_hbm, d_hbm, col_ref, row_ref, cot_hbm,
    hid_hbm, wg_hbm, fg_hbm,
    feat, w, d, cot, own, xs, cols, scales, deg1, deg2, rdeg, hT, part, e1, e2s, e2r, tot,
    hid, pushed, pushT, tt, bx1, bx2, u, fin, g, w1, g1, w2, g2, w3, g3, g4, gout, fg,
    in_sem, out_sem, s1_s, s1_r, x_s, x_r, d1_s, d1_r, d2_s, d2_r, rd_s, rd_r,
    e_s, e_r, b_s, b_r, f_s, f_r, w1_s, w1_r, w2_s, w2_r, w3_s, w3_r, w4_s, w4_r, w5_s, w5_r,
):
    row = lax.axis_index("row")
    q = lax.axis_index("rep")
    y = (row // 16) * 2 + q // 2
    x = (row // 4) % 4
    z = row % 4
    c = q % 2
    yh = row // 16
    yl = q // 2
    zp = z + 4 - q
    me8 = yh * 4 + q
    sent = []

    def remote(src, dst, ssem, rsem, to):
        return pltpu.make_async_remote_copy(
            src_ref=src, dst_ref=dst, send_sem=ssem, recv_sem=rsem, device_id=to, device_id_type=MESH
        )

    def send(src, dst, ssem, rsem, to):
        copy = remote(src, dst, ssem, rsem, to)
        copy.start()
        sent.append(copy)
        return copy

    loads = [
        pltpu.make_async_copy(src, dst, in_sem.at[n])
        for n, (src, dst) in enumerate(((feat_hbm, feat), (d_hbm, d), (w_hbm, w), (cot_hbm, cot)))
    ]
    for copy in loads:
        copy.start()

    barrier = pltpu.get_barrier_semaphore()
    place32 = y * 8 + z * 2 + c
    for n in range(1, 32):
        other = (place32 + n) % 32
        pl.semaphore_signal(
            barrier, inc=1, device_id=place(other // 8, x, (other // 2) % 4, other % 2), device_id_type=MESH
        )
    for n in range(1, 4):
        pl.semaphore_signal(barrier, inc=1, device_id=place(y, x + n, z, c), device_id_type=MESH)

    loads[0].wait()
    key0, key1 = key_ref[0], key_ref[1]
    for i in range(4):
        nodes = row * ROWS + i * BLK + lax.broadcasted_iota(jnp.int32, (BLK, FEAT), 0)
        feats = lax.broadcasted_iota(jnp.int32, (BLK, FEAT), 1)
        at = pl.ds(i * BLK, BLK)
        kept = keep_mask(nodes, feats, key0, key1)
        own[at, :] = jnp.where(kept, feat[at, :].astype(F32), 0.0).astype(BF16)
    cols[...] = col_ref[...]
    pl.semaphore_wait(barrier, 34)

    d1 = [
        send(cols, deg1.at[n - 1], d1_s.at[n - 1], d1_r.at[n - 1], place(y, x + n, z, c))
        for n in range(1, 4)
    ]
    rdeg[0] = row_ref[...]
    rd = []
    for n in range(1, 4):
        other = (q + n) % 4
        rd.append(send(rdeg.at[0], rdeg.at[n], rd_s.at[n - 1], rd_r.at[n - 1], (row, other)))

    to_same = remote(own, xs.at[yh * 4 + x], s1_s.at[0], s1_r.at[0], place(y, x, z + q, c))
    q_flip = 2 * (1 - yl) + c

    @pl.when(q != 0)
    def _():
        to_same.start()

    flip = send(own, xs.at[yh * 4 + x], s1_s.at[1], s1_r.at[1], place(3 - y, x, z + q_flip, c))

    @pl.when(q == 0)
    def _():
        xs[yh * 4 + x] = own[...]

    @pl.when(q != 0)
    def _():
        to_same.wait_recv()

    right, left = place(y, x + 1, z, c), place(y, x + 3, z, c)

    def hop(panel, n, to):
        return send(xs.at[panel], xs.at[panel], x_s.at[n], x_r.at[n], to)

    same, other = yh * 4 + x, (1 - yh) * 4 + x
    xr, xl = (x + 1) % 4, (x + 3) % 4
    same_right = hop(same, 0, right)
    same_left = hop(same, 1, left)
    flip.wait_recv()
    other_right = hop(other, 2, right)
    other_left = hop(other, 3, left)

    for copy in d1:
        copy.wait_recv()
    colx = cols[...] + deg1[0] + deg1[1] + deg1[2]
    deg2[0] = colx
    d2 = []
    for n in range(1, 8):
        o = (me8 + n) % 8
        o_q = o % 4
        to = place((o // 4) * 2 + o_q // 2, x, zp + o_q, o_q % 2)
        d2.append(send(deg2.at[0], deg2.at[n], d2_s.at[n - 1], d2_r.at[n - 1], to))

    same_right.wait_recv()
    far_right = hop(yh * 4 + xl, 4, right)
    other_left.wait_recv()
    far_left = hop((1 - yh) * 4 + xr, 5, left)

    for copy in d2:
        copy.wait_recv()
    total = deg2[0]
    for n in range(1, 8):
        total = total + deg2[n]
    scales[...] = lax.rsqrt(1.0 + total)
    for copy in rd:
        copy.wait_recv()
    by_rep = [rdeg[(q + 4 - s) % 4] for s in range(4)]
    row_total = (by_rep[0] + by_rep[1]) + (by_rep[2] + by_rep[3])
    row_scale = lax.rsqrt(1.0 + row_total)
    row_cols = jnp.concatenate([row_scale, row_scale], axis=0).T

    loads[1].wait()
    eye = lax.broadcasted_iota(jnp.int32, (BLK, BLK), 0) == lax.broadcasted_iota(jnp.int32, (BLK, BLK), 1)
    eye = jnp.where(eye, 1.0, 0.0)
    for l in range(32):
        flag = jnp.where(jnp.logical_and(q == 0, yh * 4 + x == l // 4), 1.0, 0.0)
        scale = scales[pl.ds(l, 1), :]
        for i in range(4):
            block = d[pl.ds(i * BLK, BLK), pl.ds(l * BLK, BLK)].astype(F32)
            if i == l % 4:
                block = block + eye * flag
            d[pl.ds(i * BLK, BLK), pl.ds(l * BLK, BLK)] = (block * scale).astype(BF16)

    def panel_cols(p):
        return pl.ds(pl.multiple_of(p * ROWS, ROWS), ROWS)

    def term(p):
        return jnp.dot(d[:, panel_cols(p)], xs[p], preferred_element_type=F32)

    acc = term(same) + term(other)
    acc = acc + term(yh * 4 + xl)
    acc = acc + term((1 - yh) * 4 + xr)
    same_left.wait_recv()
    acc = acc + term(yh * 4 + xr)
    other_right.wait_recv()
    acc = acc + term((1 - yh) * 4 + xl)
    xo = (x + 2) % 4
    far_right.wait_recv()
    acc = acc + term(yh * 4 + xo)
    far_left.wait_recv()
    acc = acc + term((1 - yh) * 4 + xo)
    h = acc.astype(BF16)
    loads[2].wait()
    part[...] = (jnp.dot(h, w[...], preferred_element_type=F32) * 1.25).astype(BF16)

    half = ROWS // 2
    mine = pl.ds(pl.multiple_of(c * half, half), half)
    theirs = pl.ds(pl.multiple_of((1 - c) * half, half), half)
    partner = place(y, x, z, 1 - c)
    e1_copy = send(part.at[theirs], e1, e_s.at[0], e_r.at[0], partner)
    hT[...] = acc.T.astype(BF16)
    e1_copy.wait_recv()
    e2s[...] = (part[mine, :].astype(F32) + e1[...].astype(F32)).astype(BF16)
    e2_copy = send(e2s, e2r, e_s.at[1], e_r.at[1], (row, (1 - yl) * 2 + c))
    e2_copy.wait_recv()
    tot[mine, :] = (e2s[...].astype(F32) + e2r[...].astype(F32)).astype(BF16)
    e3_copy = send(tot.at[mine], tot.at[mine], e_s.at[2], e_r.at[2], partner)
    loads[3].wait()
    e3_copy.wait_recv()

    for i in range(4):
        at = pl.ds(i * BLK, BLK)
        r = row_cols[:, i : i + 1]
        pre = tot[at, :].astype(F32) * r
        s = 1.0 / (1.0 + jnp.exp(-pre))
        hid[at, :] = (pre * s).astype(BF16)
        grad = cot[at, :].astype(F32) * s * (1.0 + pre * (1.0 - s)) * r
        pushed[at, :] = grad.astype(BF16)
        pushT[:, at] = grad.T.astype(BF16)
    hid_out = pltpu.make_async_copy(hid, hid_hbm, out_sem.at[0])
    hid_out.start()

    def back(p):
        out = jnp.dot(pushT[...], d[:, panel_cols(p)], preferred_element_type=F32).astype(BF16)
        for j in range(4):
            tt[p, j] = out[:, j * BLK : (j + 1) * BLK]

    back(xo)
    far0 = send(tt.at[xo], bx1.at[0], b_s.at[0], b_r.at[0], right)
    back(4 + xo)
    far1 = send(tt.at[4 + xo], bx1.at[1], b_s.at[1], b_r.at[1], left)
    back(4 + xr)
    near1r = send(tt.at[4 + xr], bx2.at[1], b_s.at[2], b_r.at[2], right)
    back(xl)
    near0l = send(tt.at[xl], bx2.at[2], b_s.at[3], b_r.at[3], left)
    back(xr)
    back(4 + xl)
    g[...] = jnp.dot(hT[...], pushed[...], preferred_element_type=F32) * 1.25
    wx = []
    for n in range(1, 4):
        xt = (x + n) % 4
        rows = pl.ds(pl.multiple_of(xt * 64, 64), 64)
        wx.append(send(g.at[rows], w1.at[n - 1], w1_s.at[n - 1], w1_r.at[n - 1], place(y, xt, z, c)))
    far0.wait_recv()
    tt[xr] = (tt[xr].astype(F32) + bx1[0].astype(F32)).astype(BF16)
    near0r = send(tt.at[xr], bx2.at[0], b_s.at[4], b_r.at[4], right)
    far1.wait_recv()
    tt[4 + xl] = (tt[4 + xl].astype(F32) + bx1[1].astype(F32)).astype(BF16)
    near1l = send(tt.at[4 + xl], bx2.at[3], b_s.at[5], b_r.at[5], left)
    back(x)
    back(4 + x)

    place8 = y * 2 + c
    for copy in wx:
        copy.wait_recv()
    rows = pl.ds(pl.multiple_of(x * 64, 64), 64)
    g1[...] = g[rows, :] + w1[0] + w1[1] + w1[2]
    w2c = []
    for n in range(1, 8):
        o = (place8 + n) % 8
        src = g1.at[pl.ds(pl.multiple_of(o * 8, 8), 8)]
        w2c.append(send(src, w2.at[n - 1], w2_s.at[n - 1], w2_r.at[n - 1], place(o // 2, x, z, o % 2)))

    near0l.wait_recv()
    near0r.wait_recv()
    near1r.wait_recv()
    near1l.wait_recv()
    fins = []
    for h2 in range(2):
        p = h2 * 4 + x
        left_in, right_in = (bx2[0], bx2[2]) if h2 == 0 else (bx2[1], bx2[3])
        u[h2] = (tt[p].astype(F32) + left_in.astype(F32) + right_in.astype(F32)).astype(BF16)
        for j in range(4):
            n = h2 * 4 + j
            copy = remote(
                u.at[h2, j], fin.at[me8], f_s.at[n], f_r.at[me8], place(2 * h2 + j // 2, x, zp, j % 2)
            )
            if j == 0:
                is_self = jnp.logical_and(q == 0, yh == h2)

                @pl.when(jnp.logical_not(is_self))
                def _():
                    copy.start()

                @pl.when(is_self)
                def _():
                    fin[me8] = u[h2, 0]
            else:
                copy.start()
            fins.append(copy)

    for copy in w2c:
        copy.wait_recv()
    g2v = g1[pl.ds(pl.multiple_of(place8 * 8, 8), 8), :]
    for n in range(7):
        g2v = g2v + w2[n]
    g2[...] = g2v
    w3[z] = g2v
    w3c = []
    for n in range(1, 4):
        w3c.append(send(g2, w3.at[z], w3_s.at[n - 1], w3_r.at[n - 1], place(y, x, z + n, c)))
    for copy in w3c:
        copy.wait_recv()
    g4_at = pl.ds(pl.multiple_of(place8 * 8, 8), 8)
    g4[g4_at, :] = (w3[0] + w3[1]) + (w3[2] + w3[3])
    w4c = []
    for n in range(1, 8):
        o = (place8 + n) % 8
        w4c.append(
            send(g4.at[g4_at], g4.at[g4_at], w4_s.at[n - 1], w4_r.at[n - 1], place(o // 2, x, z, o % 2))
        )
    for copy in w4c:
        copy.wait_recv()
    gout[rows, :] = g4[...]
    w5c = []
    for n in range(1, 4):
        w5c.append(send(g4, gout.at[rows], w5_s.at[n - 1], w5_r.at[n - 1], place(y, x + n, z, c)))

    for n in range(8):
        copy = remote(u.at[0, 0], fin.at[n], f_s.at[n], f_r.at[n], (row, q))
        if n % 4 == 0:

            @pl.when(jnp.logical_not(jnp.logical_and(q == 0, yh == n // 4)))
            def _():
                copy.wait_recv()
        else:
            copy.wait_recv()
    proj = fin[0].astype(F32)
    for n in range(1, 8):
        proj = proj + fin[n].astype(F32)
    proj = proj.T.astype(BF16)
    back_proj = lax.dot_general(proj, w[...], (((1,), (1,)), ((), ())), preferred_element_type=F32) * 1.25
    nodes = row * ROWS + q * BLK + lax.broadcasted_iota(jnp.int32, (BLK, FEAT), 0)
    feats = lax.broadcasted_iota(jnp.int32, (BLK, FEAT), 1)
    fg[...] = jnp.where(keep_mask(nodes, feats, key0, key1), back_proj, 0.0).astype(BF16)
    fg_out = pltpu.make_async_copy(fg, fg_hbm, out_sem.at[1])
    fg_out.start()
    for copy in w5c:
        copy.wait_recv()
    wg_out = pltpu.make_async_copy(gout, wg_hbm, out_sem.at[2])
    wg_out.start()

    @pl.when(q != 0)
    def _():
        to_same.wait_send()

    for copy in sent:
        copy.wait_send()
    for n, copy in enumerate(fins):
        if n % 4 == 0:

            @pl.when(jnp.logical_not(jnp.logical_and(q == 0, yh == n // 4)))
            def _():
                copy.wait_send()
        else:
            copy.wait_send()
    hid_out.wait()
    fg_out.wait()
    wg_out.wait()


def layer(drop_key, features, weight, d, col, row, cotangent):
    dma = pltpu.SemaphoreType.DMA
    vmem = pltpu.VMEM
    any_spec = pl.BlockSpec(memory_space=pl.ANY)
    vmem_spec = pl.BlockSpec(memory_space=pltpu.VMEM)
    return pl.pallas_call(
        layer_kernel,
        out_shape=[
            jax.ShapeDtypeStruct((ROWS, FEAT), BF16),
            jax.ShapeDtypeStruct((FEAT, FEAT), F32),
            jax.ShapeDtypeStruct((BLK, FEAT), BF16),
        ],
        in_specs=[
            pl.BlockSpec(memory_space=pltpu.SMEM),
            any_spec, any_spec, any_spec, vmem_spec, vmem_spec, any_spec,
        ],
        out_specs=[any_spec, any_spec, any_spec],
        scratch_shapes=[
            vmem((ROWS, FEAT), BF16),
            vmem((FEAT, FEAT), BF16),
            vmem((ROWS, 32 * BLK), BF16),
            vmem((ROWS, FEAT), BF16),
            vmem((ROWS, FEAT), BF16),
            vmem((8, ROWS, FEAT), BF16),
            vmem((32, BLK), F32),
            vmem((32, BLK), F32),
            vmem((3, 32, BLK), F32),
            vmem((8, 32, BLK), F32),
            vmem((4, 4, BLK), F32),
            vmem((FEAT, ROWS), BF16),
            vmem((ROWS, FEAT), BF16),
            vmem((ROWS // 2, FEAT), BF16),
            vmem((ROWS // 2, FEAT), BF16),
            vmem((ROWS // 2, FEAT), BF16),
            vmem((ROWS, FEAT), BF16),
            vmem((ROWS, FEAT), BF16),
            vmem((ROWS, FEAT), BF16),
            vmem((FEAT, ROWS), BF16),
            vmem((8, 4, FEAT, BLK), BF16),
            vmem((2, 4, FEAT, BLK), BF16),
            vmem((4, 4, FEAT, BLK), BF16),
            vmem((2, 4, FEAT, BLK), BF16),
            vmem((8, FEAT, BLK), BF16),
            vmem((FEAT, FEAT), F32),
            vmem((3, 64, FEAT), F32),
            vmem((64, FEAT), F32),
            vmem((7, 8, FEAT), F32),
            vmem((8, FEAT), F32),
            vmem((4, 8, FEAT), F32),
            vmem((8, FEAT), F32),
            vmem((64, FEAT), F32),
            vmem((FEAT, FEAT), F32),
            vmem((BLK, FEAT), BF16),
            dma((4,)), dma((3,)), dma((2,)), dma((2,)), dma((6,)), dma((6,)),
            dma((3,)), dma((3,)), dma((7,)), dma((7,)), dma((3,)), dma((3,)),
            dma((3,)), dma((3,)), dma((6,)), dma((6,)), dma((8,)), dma((8,)),
            dma((3,)), dma((3,)), dma((7,)), dma((7,)), dma((3,)), dma((3,)),
            dma((7,)), dma((7,)), dma((3,)), dma((3,)),
        ],
        compiler_params=pltpu.CompilerParams(
            collective_id=0, has_side_effects=True, vmem_limit_bytes=48 << 20
        ),
        name="layer",
    )(drop_key, features, weight, d, col, row, cotangent)


def shards(features, weight, adj_tiles, block_cols, edge_keep, drop_key, cotangent):
    idx = (block_cols // 16) * 4 + block_cols % 4
    d, col, row = build(idx, edge_keep, adj_tiles)
    hidden, weight_grad, feature_grad = layer(drop_key, features, weight, d, col, row, cotangent)
    return (hidden, weight_grad, feature_grad)


def solution(mesh):
    in_specs = (
        P("row", None),
        P(),
        P("row", "rep", None, None),
        P("row", "rep"),
        P("row", "rep"),
        P(),
        P("row", None),
    )
    out_specs = (P("row", None), P(), P(("row", "rep"), None))
    return jax.shard_map(shards, mesh=mesh, in_specs=in_specs, out_specs=out_specs, check_vma=False)
```

```python
import functools

import jax
import jax.numpy as jnp
from jax import lax
from jax.experimental import pallas as pl
from jax.experimental.pallas import tpu as pltpu
from jax.sharding import PartitionSpec as P

MESH = pl.DeviceIdType.MESH
BLK = 128
FEAT = 256
ROWS = 512
CHUNKS = 4
F32 = jnp.float32
BF16 = jnp.bfloat16


def keep_mask(node_ids, feat_ids, key0, key1):
    mixed = node_ids * 73856093 ^ feat_ids * 19349663 ^ key0 * 83492791 ^ key1
    mixed = mixed ^ lax.shift_right_logical(mixed, jnp.int32(13))
    mixed = mixed * 1274126177
    mixed = mixed ^ lax.shift_right_logical(mixed, jnp.int32(16))
    return mixed & 1023 < 819


def place(y, x, z, c):
    y, x, z = y % 4, x % 4, z % 4
    return ((y // 2) * 16 + x * 4 + z, (y % 2) * 2 + c)


def build_kernel(blk_ref, keep_ref, tiles_ref, d_ref, col_ref, row_ref):
    i = pl.program_id(0)

    @pl.when(i == 0)
    def _():
        col_ref[...] = jnp.zeros_like(col_ref)

    d_ref[...] = jnp.zeros_like(d_ref)
    row_acc = jnp.zeros((BLK, BLK), F32)
    for k in range(16):
        col = blk_ref[i, k]
        slot = (col >> 4) * 4 + (col & 3)
        tile = tiles_ref[0, k].astype(F32) * keep_ref[i, k].astype(F32)
        at = pl.ds(pl.multiple_of(slot * BLK, BLK), BLK)
        d_ref[:, at] = (d_ref[:, at].astype(F32) + tile).astype(BF16)
        col_ref[pl.ds(slot, 1), :] += jnp.sum(tile, axis=0, keepdims=True)
        row_acc = row_acc + tile
    row_ref[pl.ds(i, 1), :] = jnp.sum(row_acc.T, axis=0, keepdims=True)


def build(cols, keep, tiles):
    return pl.pallas_call(
        build_kernel,
        grid_spec=pltpu.PrefetchScalarGridSpec(
            num_scalar_prefetch=2,
            grid=(4,),
            in_specs=[pl.BlockSpec((1, 16, BLK, BLK), lambda i, a, b: (i, 0, 0, 0))],
            out_specs=[
                pl.BlockSpec((BLK, 32 * BLK), lambda i, a, b: (i, 0)),
                pl.BlockSpec((32, BLK), lambda i, a, b: (0, 0)),
                pl.BlockSpec((4, BLK), lambda i, a, b: (0, 0)),
            ],
        ),
        out_shape=[
            jax.ShapeDtypeStruct((ROWS, 32 * BLK), BF16),
            jax.ShapeDtypeStruct((32, BLK), F32),
            jax.ShapeDtypeStruct((4, BLK), F32),
        ],
        name="build",
    )(cols, keep, tiles)


def layer_kernel(
    key_ref, feat_hbm, w_hbm, d_hbm, col_ref, row_ref, cot_hbm,
    hid_hbm, wg_hbm, fg_hbm,
    feat, w, d, cot, own, xs, cols, scales, deg1, deg2, rdeg, rsc, hs, hT, part, e1, e2s, e2r, tot,
    hid, pushed, pushT, tt, zb, bfar, bnear, bside, u, yp, us, fin, g, w1, g1, w2, g2, w3, g4, gout, fg,
    in_sem, out_sem, s1_s, s1_r, x_s, x_r, z_s, z_r, d1_s, d1_r, d2_s, d2_r, rd_s, rd_r,
    e_s, e_r, zb_s, zb_r, b_s, b_r, yp_s, yp_r, f_s, f_r,
    w1_s, w1_r, w2_s, w2_r, w3_s, w3_r, w4_s, w4_r, w5_s, w5_r,
):
    row = lax.axis_index("row")
    q = lax.axis_index("rep")
    y = (row // 16) * 2 + q // 2
    x = (row // 4) % 4
    z = row % 4
    c = q % 2
    yh = row // 16
    yl = q // 2
    zp = z + 4 - q
    me8 = yh * 4 + q
    sent = []

    def remote(src, dst, ssem, rsem, to):
        return pltpu.make_async_remote_copy(
            src_ref=src, dst_ref=dst, send_sem=ssem, recv_sem=rsem, device_id=to, device_id_type=MESH
        )

    def send(src, dst, ssem, rsem, to, when=None):
        copy = remote(src, dst, ssem, rsem, to)
        if when is None:
            copy.start()
        else:
            pl.when(when)(copy.start)
        sent.append((copy, when))
        return copy

    loads = [
        pltpu.make_async_copy(src, dst, in_sem.at[n])
        for n, (src, dst) in enumerate(((feat_hbm, feat), (d_hbm, d), (w_hbm, w), (cot_hbm, cot)))
    ]
    for copy in loads:
        copy.start()

    barrier = pltpu.get_barrier_semaphore()
    place32 = y * 8 + z * 2 + c
    for n in range(1, 32):
        other = (place32 + n) % 32
        pl.semaphore_signal(
            barrier, inc=1, device_id=place(other // 8, x, (other // 2) % 4, other % 2), device_id_type=MESH
        )
    for n in range(1, 4):
        pl.semaphore_signal(barrier, inc=1, device_id=place(y, x + n, z, c), device_id_type=MESH)

    loads[0].wait()
    key0, key1 = key_ref[0], key_ref[1]
    for i in range(4):
        nodes = row * ROWS + i * BLK + lax.broadcasted_iota(jnp.int32, (BLK, FEAT), 0)
        feats = lax.broadcasted_iota(jnp.int32, (BLK, FEAT), 1)
        at = pl.ds(i * BLK, BLK)
        kept = keep_mask(nodes, feats, key0, key1)
        own[at, :] = jnp.where(kept, feat[at, :].astype(F32), 0.0).astype(BF16)
    cols[...] = col_ref[...]
    rdeg[0] = row_ref[...]
    pl.semaphore_wait(barrier, 34)

    same, other = yh * 4, 4 - yh * 4
    lead = ((yh + c) % 2) * 4
    rest = 4 - lead
    x1, x2, xo = (x + 1 + 2 * c) % 4, (x + 3 + 2 * c) % 4, (x + 2) % 4
    dev1, dev2 = place(y, x1, z, c), place(y, x2, z, c)
    pair = place(y, x, z + 1 + 2 * c, 1 - c)
    step = ROWS // CHUNKS

    def piece(panel, k):
        return xs.at[panel, pl.ds(k * step, step)]

    def own_piece(k):
        return own.at[pl.ds(k * step, step)]

    chunks = range(CHUNKS)
    got_same = [
        send(own_piece(k), piece(same + x, k), s1_s.at[0, k], s1_r.at[0, k], place(y, x, z + q, c), q != 0)
        for k in chunks
    ]
    got_other = [
        send(own_piece(k), piece(same + x, k), s1_s.at[1, k], s1_r.at[1, k], place(3 - y, x, z + c, c), yl == 1)
        for k in chunks
    ]

    d1 = [
        send(cols, deg1.at[n - 1], d1_s.at[n - 1], d1_r.at[n - 1], place(y, x + n, z, c))
        for n in range(1, 4)
    ]
    rd = [
        send(rdeg.at[0], rdeg.at[n], rd_s.at[n - 1], rd_r.at[n - 1], (row, (q + n) % 4))
        for n in range(1, 4)
    ]

    @pl.when(q == 0)
    def _():
        xs[same + x] = own[...]

    def wait_when(copy, when):
        pl.when(when)(copy.wait_recv)

    by1, by2 = [[], []], []
    for k in chunks:
        wait_when(got_same[k], q != 0)
        src = piece(same + x, k)
        send(src, src, s1_s.at[2, k], s1_r.at[1, k], place(y + 2, x, z, c), yl == 1)
        by2.append(send(src, src, x_s.at[2, k], x_r.at[2, k], dev2, c == 0))
        by1[0].append(send(src, src, x_s.at[0, k], x_r.at[0, k], dev1))
    for k in chunks:
        got_other[k].wait_recv()
        src = piece(other + x, k)
        send(src, src, x_s.at[2, k], x_r.at[2, k], dev2, c == 1)
        by1[1].append(send(src, src, x_s.at[1, k], x_r.at[1, k], dev1))

    for copy in d1:
        copy.wait_recv()
    deg2[0] = cols[...] + deg1[0] + deg1[1] + deg1[2]
    d2 = []
    for n in range(1, 8):
        o = (me8 + n) % 8
        o_q = o % 4
        to = place((o // 4) * 2 + o_q // 2, x, zp + o_q, o_q % 2)
        d2.append(send(deg2.at[0], deg2.at[n], d2_s.at[n - 1], d2_r.at[n - 1], to))

    onward, cross = [], [[], []]
    for k in chunks:
        by2[k].wait_recv()
        src = piece(lead + x1, k)
        onward.append(send(src, src, x_s.at[3, k], x_r.at[3, k], dev2))
    for k in chunks:
        src = piece(lead + x2, k)
        remote(src, src, x_s.at[0, k], x_r.at[c, k], dev1).wait_recv()
        cross[0].append(send(src, src, z_s.at[0, k], z_r.at[0, k], pair))

    for copy in rd:
        copy.wait_recv()
    by_rep = [rdeg[(q + 4 - s) % 4] for s in range(4)]
    row_scale = lax.rsqrt(1.0 + ((by_rep[0] + by_rep[1]) + (by_rep[2] + by_rep[3])))
    row_cols = jnp.concatenate([row_scale, row_scale], axis=0).T
    for i in range(4):
        rsc[i] = row_cols[:, i : i + 1]
    for copy in d2:
        copy.wait_recv()
    total = deg2[0]
    for n in range(1, 8):
        total = total + deg2[n]
    scales[...] = lax.rsqrt(1.0 + total)

    loads[1].wait()
    eye = lax.broadcasted_iota(jnp.int32, (BLK, BLK), 0) == lax.broadcasted_iota(jnp.int32, (BLK, BLK), 1)
    eye = jnp.where(eye, 1.0, 0.0)
    for l in range(32):
        flag = jnp.where(jnp.logical_and(q == 0, same + x == l // 4), 1.0, 0.0)
        scale = scales[pl.ds(l, 1), :]
        for i in range(4):
            block = d[pl.ds(i * BLK, BLK), pl.ds(l * BLK, BLK)].astype(F32)
            if i == l % 4:
                block = block + eye * flag
            d[pl.ds(i * BLK, BLK), pl.ds(l * BLK, BLK)] = (block * scale).astype(BF16)

    for k in chunks:
        onward[k].wait_recv()
        src = piece(lead + xo, k)
        cross[1].append(send(src, src, z_s.at[1, k], z_r.at[1, k], pair))

    def panel_cols(p):
        return pl.ds(pl.multiple_of(p * ROWS, ROWS), ROWS)

    def term(p):
        return jnp.dot(d[:, panel_cols(p)], xs[p], preferred_element_type=F32)

    acc = term(same + x) + term(other + x)
    acc = acc + term(lead + x1)
    acc = acc + term(lead + x2)
    acc = acc + term(lead + xo)
    for k in chunks:
        src = piece(rest + x2, k)
        remote(src, src, x_s.at[0, k], x_r.at[1 - c, k], dev1).wait_recv()
    acc = acc + term(rest + x2)
    for k in chunks:
        cross[0][k].wait_recv()
    acc = acc + term(rest + x1)
    for k in chunks:
        cross[1][k].wait_recv()
    acc = acc + term(rest + xo)
    hs[...] = acc.astype(BF16)
    loads[2].wait()

    half = ROWS // 2
    partner = place(y, x, z, 1 - c)
    chip = (row, (1 - yl) * 2 + c)

    def rows128(b):
        return pl.ds(pl.multiple_of(b * BLK, BLK), BLK)

    def project(b):
        part[rows128(b), :] = (
            jnp.dot(hs[rows128(b), :], w[...], preferred_element_type=F32) * 1.25
        ).astype(BF16)

    ec = [[], [], []]
    for b in range(2):
        project((1 - c) * 2 + b)
        ec[0].append(send(part.at[rows128((1 - c) * 2 + b)], e1.at[b], e_s.at[0, b], e_r.at[0, b], partner))
    project(c * 2)
    project(c * 2 + 1)
    for b in range(2):
        ec[0][b].wait_recv()
        e2s[b] = (part[rows128(c * 2 + b), :].astype(F32) + e1[b].astype(F32)).astype(BF16)
        ec[1].append(send(e2s.at[b], e2r.at[b], e_s.at[1, b], e_r.at[1, b], chip))
    hT[...] = acc.T.astype(BF16)
    loads[3].wait()

    def activate(i):
        at = rows128(i)
        r = rsc[i]
        pre = tot[at, :].astype(F32) * r
        s = 1.0 / (1.0 + jnp.exp(-pre))
        hid[at, :] = (pre * s).astype(BF16)
        grad = cot[at, :].astype(F32) * s * (1.0 + pre * (1.0 - s)) * r
        pushed[at, :] = grad.astype(BF16)
        pushT[:, at] = grad.T.astype(BF16)

    for b in range(2):
        ec[1][b].wait_recv()
        at = rows128(c * 2 + b)
        tot[at, :] = (e2s[b].astype(F32) + e2r[b].astype(F32)).astype(BF16)
        ec[2].append(send(tot.at[at], tot.at[at], e_s.at[2, b], e_r.at[2, b], partner))
    activate(c * 2)
    activate(c * 2 + 1)
    for b in range(2):
        ec[2][b].wait_recv()
        activate((1 - c) * 2 + b)
    hid_out = pltpu.make_async_copy(hid, hid_hbm, out_sem.at[0])
    hid_out.start()

    g[...] = jnp.dot(hT[...], pushed[...], preferred_element_type=F32) * 1.25
    place8 = y * 2 + c
    w1c = []
    for n in range(1, 8):
        o = (place8 + n) % 8
        src = g.at[pl.ds(pl.multiple_of(o * 32, 32), 32)]
        w1c.append(send(src, w1.at[n - 1], w1_s.at[n - 1], w1_r.at[n - 1], place(o // 2, x, z, o % 2)))

    def back(p):
        out = jnp.dot(pushT[...], d[:, panel_cols(p)], preferred_element_type=F32).astype(BF16)
        for j in range(4):
            tt[p, j] = out[:, j * BLK : (j + 1) * BLK]

    def add(*blocks):
        out = blocks[0].astype(F32)
        for block in blocks[1:]:
            out = out + block.astype(F32)
        return out.astype(BF16)

    blocks4 = range(4)
    zc, sidec, farc, nearc = [[], []], [[], []], [], []
    back(rest + xo)
    for j in blocks4:
        zc[0].append(send(tt.at[rest + xo, j], zb.at[0, j], zb_s.at[0, j], zb_r.at[0, j], pair))
    back(rest + x1)
    for j in blocks4:
        zc[1].append(send(tt.at[rest + x1, j], zb.at[1, j], zb_s.at[1, j], zb_r.at[1, j], pair))
    back(rest + x2)
    for j in blocks4:
        sidec[1].append(send(tt.at[rest + x2, j], bside.at[1, j], b_s.at[1, j], b_r.at[1, j], dev2))
    back(lead + xo)
    for j in blocks4:
        zc[0][j].wait_recv()
        tt[lead + xo, j] = add(tt[lead + xo, j], zb[0, j])
        farc.append(send(tt.at[lead + xo, j], bfar.at[j], b_s.at[2, j], b_r.at[2, j], dev1))
    back(lead + x2)
    for j in blocks4:
        zc[1][j].wait_recv()
        tt[lead + x2, j] = add(tt[lead + x2, j], zb[1, j])
        sidec[0].append(send(tt.at[lead + x2, j], bside.at[0, j], b_s.at[0, j], b_r.at[0, j], dev2))

    for copy in w1c:
        copy.wait_recv()
    at32 = pl.ds(pl.multiple_of(place8 * 32, 32), 32)
    out = g[at32, :]
    for n in range(7):
        out = out + w1[n]
    g1[...] = out
    w2c = []
    for n in range(1, 4):
        xt = (x + n) % 4
        src = g1.at[pl.ds(pl.multiple_of(xt * 8, 8), 8)]
        w2c.append(send(src, w2.at[n - 1], w2_s.at[n - 1], w2_r.at[n - 1], place(y, xt, z, c)))

    back(lead + x1)
    for j in blocks4:
        farc[j].wait_recv()
        tt[lead + x1, j] = add(tt[lead + x1, j], bfar[j])
        nearc.append(send(tt.at[lead + x1, j], bnear.at[j], b_s.at[3, j], b_r.at[3, j], dev1))
    back(lead + x)
    back(rest + x)

    for copy in w2c:
        copy.wait_recv()
    at8 = pl.ds(pl.multiple_of(x * 8, 8), 8)
    g2v = (g1[at8, :] + w2[0]) + (w2[1] + w2[2])
    g2[...] = g2v
    w3[z] = g2v
    w3c = [send(g2, w3.at[z], w3_s.at[n - 1], w3_r.at[n - 1], place(y, x, z + n, c)) for n in range(1, 4)]

    lead_h, rest_h = lead // 4, rest // 4
    for j in blocks4:
        sidec[1][j].wait_recv()
        u[rest_h, j] = add(tt[rest + x, j], bside[1, j])
    for j in blocks4:
        sidec[0][j].wait_recv()
        nearc[j].wait_recv()
        u[lead_h, j] = add(tt[lead + x, j], bside[0, j], bnear[j])

    ypc = [send(u.at[1 - yh, j], yp.at[j], yp_s.at[j], yp_r.at[j], place(y + 2, x, z, c), yl == 1) for j in blocks4]

    for copy in w3c:
        copy.wait_recv()
    g4[at8, :] = (w3[0] + w3[1]) + (w3[2] + w3[3])
    w4c = [
        send(g4.at[at8], g4.at[at8], w4_s.at[n - 1], w4_r.at[n - 1], place(y, x + n, z, c))
        for n in range(1, 4)
    ]

    slot = jnp.where(yl == 0, yh * 2 + q, 2 + q)
    is0 = q == 0
    for j in blocks4:
        to = place(2 * (1 - yh) + j // 2, x, zp, j % 2)
        send(u.at[1 - yh, j], fin.at[slot], f_s.at[1, j], f_r.at[slot], to, yl == 0)
    for j in blocks4:
        wait_when(ypc[j], yl == 1)

        @pl.when(yl == 1)
        def _():
            us[j] = add(u[yh, j], yp[j])

        @pl.when(yl == 0)
        def _():
            us[j] = u[yh, j]

        to = place(2 * yh + j // 2, x, zp, j % 2)
        send(us.at[j], fin.at[slot], f_s.at[0, j], f_r.at[slot], to, jnp.logical_not(is0) if j == 0 else None)

    @pl.when(is0)
    def _():
        fin[slot] = us[0]

    for copy in w4c:
        copy.wait_recv()
    gout[at32, :] = g4[...]
    w5c = []
    for n in range(1, 8):
        o = (place8 + n) % 8
        w5c.append(send(g4, gout.at[at32], w5_s.at[n - 1], w5_r.at[n - 1], place(o // 2, x, z, o % 2)))

    for n in range(6):
        copy = remote(us.at[0], fin.at[n], f_s.at[0, 0], f_r.at[n], (row, q))
        if n == 0 or n == 2:
            wait_when(copy, jnp.logical_not(jnp.logical_and(is0, slot == n)))
        else:
            copy.wait_recv()
    proj = fin[0].astype(F32)
    for n in range(1, 6):
        proj = proj + fin[n].astype(F32)
    proj = proj.T.astype(BF16)
    back_proj = lax.dot_general(proj, w[...], (((1,), (1,)), ((), ())), preferred_element_type=F32) * 1.25
    nodes = row * ROWS + q * BLK + lax.broadcasted_iota(jnp.int32, (BLK, FEAT), 0)
    feats = lax.broadcasted_iota(jnp.int32, (BLK, FEAT), 1)
    fg[...] = jnp.where(keep_mask(nodes, feats, key0, key1), back_proj, 0.0).astype(BF16)
    fg_out = pltpu.make_async_copy(fg, fg_hbm, out_sem.at[1])
    fg_out.start()
    for copy in w5c:
        copy.wait_recv()
    wg_out = pltpu.make_async_copy(gout, wg_hbm, out_sem.at[2])
    wg_out.start()
    for copy, when in sent:
        if when is None:
            copy.wait_send()
        else:
            pl.when(when)(copy.wait_send)
    hid_out.wait()
    fg_out.wait()
    wg_out.wait()


def layer(drop_key, features, weight, d, col, row, cotangent):
    dma = pltpu.SemaphoreType.DMA
    vmem = pltpu.VMEM
    any_spec = pl.BlockSpec(memory_space=pl.ANY)
    vmem_spec = pl.BlockSpec(memory_space=pltpu.VMEM)
    return pl.pallas_call(
        layer_kernel,
        out_shape=[
            jax.ShapeDtypeStruct((ROWS, FEAT), BF16),
            jax.ShapeDtypeStruct((FEAT, FEAT), F32),
            jax.ShapeDtypeStruct((BLK, FEAT), BF16),
        ],
        in_specs=[
            pl.BlockSpec(memory_space=pltpu.SMEM),
            any_spec, any_spec, any_spec, vmem_spec, vmem_spec, any_spec,
        ],
        out_specs=[any_spec, any_spec, any_spec],
        scratch_shapes=[
            vmem((ROWS, FEAT), BF16),
            vmem((FEAT, FEAT), BF16),
            vmem((ROWS, 32 * BLK), BF16),
            vmem((ROWS, FEAT), BF16),
            vmem((ROWS, FEAT), BF16),
            vmem((8, ROWS, FEAT), BF16),
            vmem((32, BLK), F32),
            vmem((32, BLK), F32),
            vmem((3, 32, BLK), F32),
            vmem((8, 32, BLK), F32),
            vmem((4, 4, BLK), F32),
            vmem((4, BLK, 1), F32),
            vmem((ROWS, FEAT), BF16),
            vmem((FEAT, ROWS), BF16),
            vmem((ROWS, FEAT), BF16),
            vmem((2, BLK, FEAT), BF16),
            vmem((2, BLK, FEAT), BF16),
            vmem((2, BLK, FEAT), BF16),
            vmem((ROWS, FEAT), BF16),
            vmem((ROWS, FEAT), BF16),
            vmem((ROWS, FEAT), BF16),
            vmem((FEAT, ROWS), BF16),
            vmem((8, 4, FEAT, BLK), BF16),
            vmem((2, 4, FEAT, BLK), BF16),
            vmem((4, FEAT, BLK), BF16),
            vmem((4, FEAT, BLK), BF16),
            vmem((2, 4, FEAT, BLK), BF16),
            vmem((2, 4, FEAT, BLK), BF16),
            vmem((4, FEAT, BLK), BF16),
            vmem((4, FEAT, BLK), BF16),
            vmem((6, FEAT, BLK), BF16),
            vmem((FEAT, FEAT), F32),
            vmem((7, 32, FEAT), F32),
            vmem((32, FEAT), F32),
            vmem((3, 8, FEAT), F32),
            vmem((8, FEAT), F32),
            vmem((4, 8, FEAT), F32),
            vmem((32, FEAT), F32),
            vmem((FEAT, FEAT), F32),
            vmem((BLK, FEAT), BF16),
            dma((4,)), dma((3,)),
            dma((3, CHUNKS)), dma((2, CHUNKS)),
            dma((4, CHUNKS)), dma((4, CHUNKS)),
            dma((2, CHUNKS)), dma((2, CHUNKS)),
            dma((3,)), dma((3,)), dma((7,)), dma((7,)), dma((3,)), dma((3,)),
            dma((3, 2)), dma((3, 2)),
            dma((2, 4)), dma((2, 4)), dma((4, 4)), dma((4, 4)),
            dma((4,)), dma((4,)), dma((2, 4)), dma((6,)),
            dma((7,)), dma((7,)), dma((3,)), dma((3,)), dma((3,)), dma((3,)),
            dma((3,)), dma((3,)), dma((7,)), dma((7,)),
        ],
        compiler_params=pltpu.CompilerParams(
            collective_id=0, has_side_effects=True, vmem_limit_bytes=48 << 20
        ),
        name="layer",
    )(drop_key, features, weight, d, col, row, cotangent)


def shards(features, weight, adj_tiles, block_cols, edge_keep, drop_key, cotangent):
    d, col, row = build(block_cols, edge_keep, adj_tiles)
    hidden, weight_grad, feature_grad = layer(drop_key, features, weight, d, col, row, cotangent)
    return (hidden, weight_grad, feature_grad)


def solution(mesh):
    in_specs = (
        P("row", None),
        P(),
        P("row", "rep", None, None),
        P("row", "rep"),
        P("row", "rep"),
        P(),
        P("row", None),
    )
    out_specs = (P("row", None), P(), P(("row", "rep"), None))
    return jax.shard_map(shards, mesh=mesh, in_specs=in_specs, out_specs=out_specs, check_vma=False)
```

```python
import functools

import jax
import jax.numpy as jnp
from jax import lax
from jax.experimental import pallas as pl
from jax.experimental.pallas import tpu as pltpu
from jax.sharding import PartitionSpec as P

MESH = pl.DeviceIdType.MESH
BLK = 128
FEAT = 256
ROWS = 512
CHUNKS = 4
F32 = jnp.float32
BF16 = jnp.bfloat16


def keep_mask(node_ids, feat_ids, key0, key1):
    mixed = node_ids * 73856093 ^ feat_ids * 19349663 ^ key0 * 83492791 ^ key1
    mixed = mixed ^ lax.shift_right_logical(mixed, jnp.int32(13))
    mixed = mixed * 1274126177
    mixed = mixed ^ lax.shift_right_logical(mixed, jnp.int32(16))
    return mixed & 1023 < 819


def place(y, x, z, c):
    y, x, z = y % 4, x % 4, z % 4
    return ((y // 2) * 16 + x * 4 + z, (y % 2) * 2 + c)


def build_kernel(blk_ref, keep_ref, tiles_ref, d_ref, col_ref, row_ref):
    i = pl.program_id(0)

    @pl.when(i == 0)
    def _():
        col_ref[...] = jnp.zeros_like(col_ref)

    d_ref[...] = jnp.zeros_like(d_ref)
    row_acc = jnp.zeros((BLK, BLK), F32)
    for k in range(16):
        col = blk_ref[i, k]
        slot = (col >> 4) * 4 + (col & 3)
        tile = tiles_ref[0, k].astype(F32) * keep_ref[i, k].astype(F32)
        at = pl.ds(pl.multiple_of(slot * BLK, BLK), BLK)
        d_ref[:, at] = (d_ref[:, at].astype(F32) + tile).astype(BF16)
        col_ref[pl.ds(slot, 1), :] += jnp.sum(tile, axis=0, keepdims=True)
        row_acc = row_acc + tile
    row_ref[pl.ds(i, 1), :] = jnp.sum(row_acc.T, axis=0, keepdims=True)


def build(cols, keep, tiles):
    return pl.pallas_call(
        build_kernel,
        grid_spec=pltpu.PrefetchScalarGridSpec(
            num_scalar_prefetch=2,
            grid=(4,),
            in_specs=[pl.BlockSpec((1, 16, BLK, BLK), lambda i, a, b: (i, 0, 0, 0))],
            out_specs=[
                pl.BlockSpec((BLK, 32 * BLK), lambda i, a, b: (i, 0)),
                pl.BlockSpec((32, BLK), lambda i, a, b: (0, 0)),
                pl.BlockSpec((4, BLK), lambda i, a, b: (0, 0)),
            ],
        ),
        out_shape=[
            jax.ShapeDtypeStruct((ROWS, 32 * BLK), BF16),
            jax.ShapeDtypeStruct((32, BLK), F32),
            jax.ShapeDtypeStruct((4, BLK), F32),
        ],
        name="build",
    )(cols, keep, tiles)


def layer_kernel(
    key_ref, feat_hbm, w_hbm, d_hbm, col_ref, row_ref, cot_hbm,
    hid_hbm, wg_hbm, fg_hbm,
    feat, w, d, cot, own, xs, cols, scales, deg1, deg2, rdeg, rsc, hs, hT, part, e1, e2s, e2r, tot,
    hid, pushed, pushT, tt, zb, bfar, bnear, bside, u, yp, fin, g, w1, w2, w3, g4, fg,
    in_sem, out_sem, s1_s, s1_r, x_s, x_r, z_s, z_r, d1_s, d1_r, d2_s, d2_r, rd_s, rd_r,
    e_s, e_r, zb_s, zb_r, b_s, b_r, yp_s, yp_r, f_s, f_r,
    w1_s, w1_r, w2_s, w2_r, w3_s, w3_r, w4_s, w4_r,
):
    row = lax.axis_index("row")
    q = lax.axis_index("rep")
    y = (row // 16) * 2 + q // 2
    x = (row // 4) % 4
    z = row % 4
    c = q % 2
    yh = row // 16
    yl = q // 2
    zp = z + 4 - q
    me8 = yh * 4 + q
    sent = []

    def remote(src, dst, ssem, rsem, to):
        return pltpu.make_async_remote_copy(
            src_ref=src, dst_ref=dst, send_sem=ssem, recv_sem=rsem, device_id=to, device_id_type=MESH
        )

    def send(src, dst, ssem, rsem, to, when=None):
        copy = remote(src, dst, ssem, rsem, to)
        if when is None:
            copy.start()
        else:
            pl.when(when)(copy.start)
        sent.append((copy, when))
        return copy

    loads = [
        pltpu.make_async_copy(src, dst, in_sem.at[n])
        for n, (src, dst) in enumerate(((feat_hbm, feat), (d_hbm, d), (w_hbm, w), (cot_hbm, cot)))
    ]
    for copy in loads:
        copy.start()

    barrier = pltpu.get_barrier_semaphore()
    place32 = y * 8 + z * 2 + c
    for n in range(1, 32):
        other = (place32 + n) % 32
        pl.semaphore_signal(
            barrier, inc=1, device_id=place(other // 8, x, (other // 2) % 4, other % 2), device_id_type=MESH
        )
    for n in range(1, 4):
        pl.semaphore_signal(barrier, inc=1, device_id=place(y, x + n, z, c), device_id_type=MESH)

    loads[0].wait()
    key0, key1 = key_ref[0], key_ref[1]
    for i in range(4):
        nodes = row * ROWS + i * BLK + lax.broadcasted_iota(jnp.int32, (BLK, FEAT), 0)
        feats = lax.broadcasted_iota(jnp.int32, (BLK, FEAT), 1)
        at = pl.ds(i * BLK, BLK)
        kept = keep_mask(nodes, feats, key0, key1)
        own[at, :] = jnp.where(kept, feat[at, :].astype(F32), 0.0).astype(BF16)
    cols[...] = col_ref[...]
    rdeg[0] = row_ref[...]
    pl.semaphore_wait(barrier, 34)

    same = yh * 4
    lead = ((yh + c) % 2) * 4
    rest = 4 - lead
    x1, x2, xo = (x + 1 + 2 * c) % 4, (x + 3 + 2 * c) % 4, (x + 2) % 4
    dev1, dev2 = place(y, x1, z, c), place(y, x2, z, c)
    pair = place(y, x, z + 1 + 2 * c, 1 - c)
    step = ROWS // CHUNKS

    def piece(panel, k):
        return xs.at[panel, pl.ds(k * step, step)]

    def own_piece(k):
        return own.at[pl.ds(k * step, step)]

    chunks = range(CHUNKS)
    first = lead + x
    last = rest + x
    across = place(y + 2, x, z, c)
    to_y = jnp.where(c == 0, y, 3 - y)
    to_z = z + jnp.where(c == 0, q, 3 - 2 * yl)
    got = [
        send(own_piece(k), piece(same + x, k), s1_s.at[0, k], s1_r.at[0, k], place(to_y, x, to_z, c), q != 0)
        for k in chunks
    ]

    d1 = [
        send(cols, deg1.at[n - 1], d1_s.at[n - 1], d1_r.at[n - 1], place(y, x + n, z, c))
        for n in range(1, 4)
    ]
    rd = [
        send(rdeg.at[0], rdeg.at[n], rd_s.at[n - 1], rd_r.at[n - 1], (row, (q + n) % 4))
        for n in range(1, 4)
    ]

    @pl.when(q == 0)
    def _():
        xs[same + x] = own[...]

    loads[1].wait()

    @pl.when(q == 0)
    def _():
        eye = lax.broadcasted_iota(jnp.int32, (BLK, BLK), 0) == lax.broadcasted_iota(jnp.int32, (BLK, BLK), 1)
        eye = jnp.where(eye, 1.0, 0.0)
        for i in range(4):
            at = pl.ds(i * BLK, BLK), pl.ds(pl.multiple_of(first * ROWS + i * BLK, BLK), BLK)
            d[at] = (d[at].astype(F32) + eye).astype(BF16)

    def wait_when(copy, when):
        pl.when(when)(copy.wait_recv)

    by1, by2, got_rest = [[], []], [], []
    for k in chunks:
        wait_when(got[k], q != 0)
        src = piece(first, k)
        by2.append(send(src, src, x_s.at[2, k], x_r.at[2, k], dev2))
        by1[0].append(send(src, src, x_s.at[0, k], x_r.at[0, k], dev1))
        got_rest.append(send(src, src, s1_s.at[1, k], s1_r.at[1, k], across))

    for copy in d1:
        copy.wait_recv()
    deg2[0] = cols[...] + deg1[0] + deg1[1] + deg1[2]
    d2 = []
    for n in range(1, 8):
        o = (me8 + n) % 8
        o_q = o % 4
        to = place((o // 4) * 2 + o_q // 2, x, zp + o_q, o_q % 2)
        d2.append(send(deg2.at[0], deg2.at[n], d2_s.at[n - 1], d2_r.at[n - 1], to))

    onward, cross = [], [[], []]
    for k in chunks:
        by2[k].wait_recv()
        src = piece(lead + x1, k)
        onward.append(send(src, src, x_s.at[3, k], x_r.at[3, k], dev2))
    for k in chunks:
        by1[0][k].wait_recv()
        src = piece(lead + x2, k)
        cross[0].append(send(src, src, z_s.at[0, k], z_r.at[0, k], pair))
    for k in chunks:
        got_rest[k].wait_recv()
        src = piece(last, k)
        by1[1].append(send(src, src, x_s.at[1, k], x_r.at[1, k], dev1))

    for copy in rd:
        copy.wait_recv()
    by_rep = [rdeg[(q + 4 - s) % 4] for s in range(4)]
    row_scale = lax.rsqrt(1.0 + ((by_rep[0] + by_rep[1]) + (by_rep[2] + by_rep[3])))
    row_cols = jnp.concatenate([row_scale, row_scale], axis=0).T
    for i in range(4):
        rsc[i] = row_cols[:, i : i + 1]
    for copy in d2:
        copy.wait_recv()
    total = deg2[0]
    for n in range(1, 8):
        total = total + deg2[n]
    scales[...] = lax.rsqrt(1.0 + total)

    narrow = scales[...].astype(BF16)

    def scale_panel(p):
        for l in range(4 * p, 4 * p + 4):
            at = pl.ds(l * BLK, BLK)
            d[:, at] = d[:, at] * narrow[l : l + 1, :]

    for k in chunks:
        for p in range(8 * k // CHUNKS, 8 * (k + 1) // CHUNKS):
            scale_panel(p)
        onward[k].wait_recv()
        src = piece(lead + xo, k)
        cross[1].append(send(src, src, z_s.at[1, k], z_r.at[1, k], pair))

    def panel_cols(p):
        return pl.ds(pl.multiple_of(p * ROWS, ROWS), ROWS)

    def term(p):
        return jnp.dot(d[:, panel_cols(p)], xs[p], preferred_element_type=F32)

    acc = term(first) + term(last)
    acc = acc + term(lead + x1)
    acc = acc + term(lead + x2)
    acc = acc + term(lead + xo)
    for k in chunks:
        cross[0][k].wait_recv()
    acc = acc + term(rest + x1)
    for k in chunks:
        by1[1][k].wait_recv()
    acc = acc + term(rest + x2)
    for k in chunks:
        cross[1][k].wait_recv()
    acc = acc + term(rest + xo)
    hs[...] = acc.astype(BF16)
    loads[2].wait()

    half = ROWS // 2
    partner = place(y, x, z, 1 - c)
    chip = (row, (1 - yl) * 2 + c)

    def rows128(b):
        return pl.ds(pl.multiple_of(b * BLK, BLK), BLK)

    def project(b):
        part[rows128(b), :] = (
            jnp.dot(hs[rows128(b), :], w[...], preferred_element_type=F32) * 1.25
        ).astype(BF16)

    ec = [[], [], []]
    for b in range(2):
        project((1 - c) * 2 + b)
        ec[0].append(send(part.at[rows128((1 - c) * 2 + b)], e1.at[b], e_s.at[0, b], e_r.at[0, b], partner))
    project(c * 2)
    project(c * 2 + 1)
    for b in range(2):
        ec[0][b].wait_recv()
        e2s[b] = (part[rows128(c * 2 + b), :].astype(F32) + e1[b].astype(F32)).astype(BF16)
        ec[1].append(send(e2s.at[b], e2r.at[b], e_s.at[1, b], e_r.at[1, b], chip))
    hT[...] = acc.T.astype(BF16)
    loads[3].wait()

    def activate(i):
        at = rows128(i)
        r = rsc[i]
        pre = tot[at, :].astype(F32) * r
        s = 1.0 / (1.0 + jnp.exp(-pre))
        hid[at, :] = (pre * s).astype(BF16)
        grad = cot[at, :].astype(F32) * s * (1.0 + pre * (1.0 - s)) * r
        pushed[at, :] = grad.astype(BF16)
        pushT[:, at] = grad.T.astype(BF16)

    for b in range(2):
        ec[1][b].wait_recv()
        at = rows128(c * 2 + b)
        tot[at, :] = (e2s[b].astype(F32) + e2r[b].astype(F32)).astype(BF16)
        ec[2].append(send(tot.at[at], tot.at[at], e_s.at[2, b], e_r.at[2, b], partner))
    activate(c * 2)
    activate(c * 2 + 1)
    for b in range(2):
        ec[2][b].wait_recv()
        activate((1 - c) * 2 + b)
    hid_out = pltpu.make_async_copy(hid, hid_hbm, out_sem.at[0])
    hid_out.start()

    g[...] = (jnp.dot(hT[...], pushed[...], preferred_element_type=F32) * 1.25).astype(BF16)
    place8 = y * 2 + c
    at32 = pl.ds(pl.multiple_of(place8 * 32, 32), 32)
    w1c = []
    for n in range(1, 8):
        o = (place8 + n) % 8
        src = g.at[pl.ds(pl.multiple_of(o * 32, 32), 32)]
        w1c.append(send(src, w1.at[n - 1], w1_s.at[n - 1], w1_r.at[n - 1], place(o // 2, x, z, o % 2)))

    def back(p):
        out = jnp.dot(pushT[...], d[:, panel_cols(p)], preferred_element_type=F32).astype(BF16)
        for j in range(4):
            tt[p, j] = out[:, j * BLK : (j + 1) * BLK]

    def add(*blocks):
        out = blocks[0].astype(F32)
        for block in blocks[1:]:
            out = out + block.astype(F32)
        return out.astype(BF16)

    blocks4 = range(4)
    zc, sidec, farc, nearc = [[], []], [[], []], [], []
    back(rest + xo)
    for j in blocks4:
        zc[0].append(send(tt.at[rest + xo, j], zb.at[0, j], zb_s.at[0, j], zb_r.at[0, j], pair))
    back(rest + x1)
    for j in blocks4:
        zc[1].append(send(tt.at[rest + x1, j], zb.at[1, j], zb_s.at[1, j], zb_r.at[1, j], pair))
    back(rest + x2)
    for j in blocks4:
        sidec[1].append(send(tt.at[rest + x2, j], bside.at[1, j], b_s.at[1, j], b_r.at[1, j], dev2))
    for copy in w1c:
        copy.wait_recv()
    w2[x] = add(g[at32, :], *[w1[n] for n in range(7)])
    w2c = [
        send(w2.at[x], w2.at[x], w2_s.at[n - 1], w2_r.at[n - 1], place(y, x + n, z, c)) for n in range(1, 4)
    ]

    back(last)
    back(lead + xo)
    for j in blocks4:
        zc[0][j].wait_recv()
        tt[lead + xo, j] = add(tt[lead + xo, j], zb[0, j])
        farc.append(send(tt.at[lead + xo, j], bfar.at[j], b_s.at[2, j], b_r.at[2, j], dev1))
    back(lead + x2)
    for j in blocks4:
        zc[1][j].wait_recv()
        tt[lead + x2, j] = add(tt[lead + x2, j], zb[1, j])
        sidec[0].append(send(tt.at[lead + x2, j], bside.at[0, j], b_s.at[0, j], b_r.at[0, j], dev2))

    for copy in w2c:
        copy.wait_recv()
    w3[z] = add(w2[0], w2[1], w2[2], w2[3])
    w3c = [
        send(w3.at[z], w3.at[z], w3_s.at[n - 1], w3_r.at[n - 1], place(y, x, z + n, c)) for n in range(1, 4)
    ]

    ypc = []
    for j in blocks4:
        sidec[1][j].wait_recv()
        u[1, j] = add(tt[last, j], bside[1, j])
        ypc.append(send(u.at[1, j], yp.at[j], yp_s.at[j], yp_r.at[j], across))

    back(lead + x1)
    for j in blocks4:
        farc[j].wait_recv()
        tt[lead + x1, j] = add(tt[lead + x1, j], bfar[j])
        nearc.append(send(tt.at[lead + x1, j], bnear.at[j], b_s.at[3, j], b_r.at[3, j], dev1))
    back(first)

    for copy in w3c:
        copy.wait_recv()
    g4[at32, :] = add(w3[0], w3[1], w3[2], w3[3])
    w4c = []
    for n in range(1, 8):
        o = (place8 + n) % 8
        src = g4.at[at32]
        w4c.append(send(src, src, w4_s.at[n - 1], w4_r.at[n - 1], place(o // 2, x, z, o % 2)))

    half_of = (yh + c) % 2
    for j in blocks4:
        sidec[0][j].wait_recv()
        nearc[j].wait_recv()
        ypc[j].wait_recv()
        u[0, j] = add(tt[first, j], bside[0, j], bnear[j], yp[j])
        to = place(2 * half_of + j // 2, x, zp, j % 2)
        send(u.at[0, j], fin.at[q], f_s.at[j], f_r.at[q], to, q != 0 if j == 0 else None)

    @pl.when(q == 0)
    def _():
        fin[0] = u[0, 0]

    for n in range(4):
        copy = remote(u.at[0, 0], fin.at[n], f_s.at[0], f_r.at[n], (row, q))
        if n == 0:
            wait_when(copy, q != 0)
        else:
            copy.wait_recv()
    proj = fin[0].astype(F32)
    for n in range(1, 4):
        proj = proj + fin[n].astype(F32)
    fg[...] = proj.T.astype(BF16)
    fg_out = pltpu.make_async_copy(fg, fg_hbm, out_sem.at[1])
    fg_out.start()
    for copy in w4c:
        copy.wait_recv()
    wg_out = pltpu.make_async_copy(g4, wg_hbm, out_sem.at[2])
    wg_out.start()
    for copy, when in sent:
        if when is None:
            copy.wait_send()
        else:
            pl.when(when)(copy.wait_send)
    hid_out.wait()
    fg_out.wait()
    wg_out.wait()


def layer(drop_key, features, weight, d, col, row, cotangent):
    dma = pltpu.SemaphoreType.DMA
    vmem = pltpu.VMEM
    any_spec = pl.BlockSpec(memory_space=pl.ANY)
    vmem_spec = pl.BlockSpec(memory_space=pltpu.VMEM)
    return pl.pallas_call(
        layer_kernel,
        out_shape=[
            jax.ShapeDtypeStruct((ROWS, FEAT), BF16),
            jax.ShapeDtypeStruct((FEAT, FEAT), BF16),
            jax.ShapeDtypeStruct((BLK, FEAT), BF16),
        ],
        in_specs=[
            pl.BlockSpec(memory_space=pltpu.SMEM),
            any_spec, any_spec, any_spec, vmem_spec, vmem_spec, any_spec,
        ],
        out_specs=[any_spec, any_spec, any_spec],
        scratch_shapes=[
            vmem((ROWS, FEAT), BF16),
            vmem((FEAT, FEAT), BF16),
            vmem((ROWS, 32 * BLK), BF16),
            vmem((ROWS, FEAT), BF16),
            vmem((ROWS, FEAT), BF16),
            vmem((8, ROWS, FEAT), BF16),
            vmem((32, BLK), F32),
            vmem((32, BLK), F32),
            vmem((3, 32, BLK), F32),
            vmem((8, 32, BLK), F32),
            vmem((4, 4, BLK), F32),
            vmem((4, BLK, 1), F32),
            vmem((ROWS, FEAT), BF16),
            vmem((FEAT, ROWS), BF16),
            vmem((ROWS, FEAT), BF16),
            vmem((2, BLK, FEAT), BF16),
            vmem((2, BLK, FEAT), BF16),
            vmem((2, BLK, FEAT), BF16),
            vmem((ROWS, FEAT), BF16),
            vmem((ROWS, FEAT), BF16),
            vmem((ROWS, FEAT), BF16),
            vmem((FEAT, ROWS), BF16),
            vmem((8, 4, FEAT, BLK), BF16),
            vmem((2, 4, FEAT, BLK), BF16),
            vmem((4, FEAT, BLK), BF16),
            vmem((4, FEAT, BLK), BF16),
            vmem((2, 4, FEAT, BLK), BF16),
            vmem((2, 4, FEAT, BLK), BF16),
            vmem((4, FEAT, BLK), BF16),
            vmem((4, FEAT, BLK), BF16),
            vmem((FEAT, FEAT), BF16),
            vmem((7, 32, FEAT), BF16),
            vmem((4, 32, FEAT), BF16),
            vmem((4, 32, FEAT), BF16),
            vmem((FEAT, FEAT), BF16),
            vmem((BLK, FEAT), BF16),
            dma((4,)), dma((3,)),
            dma((2, CHUNKS)), dma((2, CHUNKS)),
            dma((4, CHUNKS)), dma((4, CHUNKS)),
            dma((2, CHUNKS)), dma((2, CHUNKS)),
            dma((3,)), dma((3,)), dma((7,)), dma((7,)), dma((3,)), dma((3,)),
            dma((3, 2)), dma((3, 2)),
            dma((2, 4)), dma((2, 4)), dma((4, 4)), dma((4, 4)),
            dma((4,)), dma((4,)), dma((4,)), dma((4,)),
            dma((7,)), dma((7,)), dma((3,)), dma((3,)), dma((3,)), dma((3,)),
            dma((7,)), dma((7,)),
        ],
        compiler_params=pltpu.CompilerParams(
            collective_id=0, has_side_effects=True, vmem_limit_bytes=58 << 20
        ),
        name="layer",
    )(drop_key, features, weight, d, col, row, cotangent)


def finish_kernel(key_ref, hid_ref, g_ref, proj_ref, w_ref, hid_out, wg_out, fg_out):
    hid_out[...] = hid_ref[...]
    wg_out[...] = g_ref[...].astype(F32)
    back_proj = (
        lax.dot_general(proj_ref[...], w_ref[...], (((1,), (1,)), ((), ())), preferred_element_type=F32) * 1.25
    )
    first = lax.axis_index("row") * ROWS + lax.axis_index("rep") * BLK
    nodes = first + lax.broadcasted_iota(jnp.int32, (BLK, FEAT), 0)
    feats = lax.broadcasted_iota(jnp.int32, (BLK, FEAT), 1)
    kept = keep_mask(nodes, feats, key_ref[0], key_ref[1])
    fg_out[...] = jnp.where(kept, back_proj, 0.0).astype(BF16)


def finish(drop_key, hid, g, proj, weight):
    return pl.pallas_call(
        finish_kernel,
        out_shape=[
            jax.ShapeDtypeStruct((ROWS, FEAT), BF16),
            jax.ShapeDtypeStruct((FEAT, FEAT), F32),
            jax.ShapeDtypeStruct((BLK, FEAT), BF16),
        ],
        in_specs=[pl.BlockSpec(memory_space=pltpu.SMEM)] + [pl.BlockSpec(memory_space=pltpu.VMEM)] * 4,
        out_specs=[pl.BlockSpec(memory_space=pltpu.VMEM)] * 3,
        name="finish",
    )(drop_key, hid, g, proj, weight)


def shards(features, weight, adj_tiles, block_cols, edge_keep, drop_key, cotangent):
    d, col, row = build(block_cols, edge_keep, adj_tiles)
    hidden, grad, proj = layer(drop_key, features, weight, d, col, row, cotangent)
    return finish(drop_key, hidden, grad, proj, weight)


def solution(mesh):
    in_specs = (
        P("row", None),
        P(),
        P("row", "rep", None, None),
        P("row", "rep"),
        P("row", "rep"),
        P(),
        P("row", None),
    )
    out_specs = (P("row", None), P(), P(("row", "rep"), None))
    return jax.shard_map(shards, mesh=mesh, in_specs=in_specs, out_specs=out_specs, check_vma=False)
```

```python
import functools

import jax
import jax.numpy as jnp
from jax import lax
from jax.experimental import pallas as pl
from jax.experimental.pallas import tpu as pltpu
from jax.sharding import PartitionSpec as P

MESH = pl.DeviceIdType.MESH
BLK = 128
FEAT = 256
ROWS = 512
CHUNKS = 4
F32 = jnp.float32
BF16 = jnp.bfloat16


def keep_mask(node_ids, feat_ids, key0, key1):
    mixed = node_ids * 73856093 ^ feat_ids * 19349663 ^ key0 * 83492791 ^ key1
    mixed = mixed ^ lax.shift_right_logical(mixed, jnp.int32(13))
    mixed = mixed * 1274126177
    mixed = mixed ^ lax.shift_right_logical(mixed, jnp.int32(16))
    return mixed & 1023 < 819


def place(y, x, z, c):
    y, x, z = y % 4, x % 4, z % 4
    return ((y // 2) * 16 + x * 4 + z, (y % 2) * 2 + c)


def build_kernel(blk_ref, keep_ref, tiles_hbm, d_ref, col_ref, row_ref, tiles, sem):
    loads = [pltpu.make_async_copy(tiles_hbm.at[i], tiles.at[i], sem.at[i]) for i in range(4)]
    for copy in loads:
        copy.start()
    col_ref[...] = jnp.zeros_like(col_ref)
    d_ref[...] = jnp.zeros_like(d_ref)
    for i in range(4):
        loads[i].wait()
        rows = pl.ds(i * BLK, BLK)
        row_acc = jnp.zeros((BLK, BLK), F32)
        for k in range(16):
            col = blk_ref[i, k]
            slot = (col >> 4) * 4 + (col & 3)
            tile = tiles[i, k] * keep_ref[i, k].astype(BF16)
            at = pl.ds(pl.multiple_of(slot * BLK, BLK), BLK)
            d_ref[rows, at] = d_ref[rows, at] + tile
            wide = tile.astype(F32)
            col_ref[pl.ds(slot, 1), :] += jnp.sum(wide, axis=0, keepdims=True)
            row_acc = row_acc + wide
        row_ref[pl.ds(i, 1), :] = jnp.sum(row_acc.T, axis=0, keepdims=True)


def build(cols, keep, tiles):
    smem, vmem = pl.BlockSpec(memory_space=pltpu.SMEM), pl.BlockSpec(memory_space=pltpu.VMEM)
    return pl.pallas_call(
        build_kernel,
        in_specs=[smem, smem, pl.BlockSpec(memory_space=pl.ANY)],
        out_specs=[vmem, vmem, vmem],
        out_shape=[
            jax.ShapeDtypeStruct((ROWS, 32 * BLK), BF16),
            jax.ShapeDtypeStruct((32, BLK), F32),
            jax.ShapeDtypeStruct((4, BLK), F32),
        ],
        scratch_shapes=[pltpu.VMEM((4, 16, BLK, BLK), BF16), pltpu.SemaphoreType.DMA((4,))],
        compiler_params=pltpu.CompilerParams(vmem_limit_bytes=12 << 20),
        name="build",
    )(cols, keep, tiles)


def layer_kernel(
    key_ref, feat_hbm, w_hbm, d_hbm, col_ref, row_ref, cot_hbm,
    hid_hbm, wg_hbm, fg_hbm,
    feat, w, d, cot, own, xs, cols, scales, deg1, deg2, rdeg, rsc, hs, hT, part, e1, e2s, e2r, tot,
    hid, pushed, pushT, tt, zb, bfar, bnear, bside, u, yp, fin, g, w1, w2, w3, g4, fg,
    in_sem, out_sem, s1_s, s1_r, x_s, x_r, z_s, z_r, d1_s, d1_r, d2_s, d2_r, rd_s, rd_r,
    e_s, e_r, zb_s, zb_r, b_s, b_r, yp_s, yp_r, f_s, f_r,
    w1_s, w1_r, w2_s, w2_r, w3_s, w3_r, w4_s, w4_r,
):
    row = lax.axis_index("row")
    q = lax.axis_index("rep")
    y = (row // 16) * 2 + q // 2
    x = (row // 4) % 4
    z = row % 4
    c = q % 2
    yh = row // 16
    yl = q // 2
    zp = z + 4 - q
    me8 = yh * 4 + q
    sent = []

    def remote(src, dst, ssem, rsem, to):
        return pltpu.make_async_remote_copy(
            src_ref=src, dst_ref=dst, send_sem=ssem, recv_sem=rsem, device_id=to, device_id_type=MESH
        )

    def send(src, dst, ssem, rsem, to, when=None):
        copy = remote(src, dst, ssem, rsem, to)
        if when is None:
            copy.start()
        else:
            pl.when(when)(copy.start)
        sent.append((copy, when))
        return copy

    loads = [
        pltpu.make_async_copy(src, dst, in_sem.at[n])
        for n, (src, dst) in enumerate(((feat_hbm, feat), (d_hbm, d), (w_hbm, w), (cot_hbm, cot)))
    ]
    for copy in loads:
        copy.start()

    barrier = pltpu.get_barrier_semaphore()
    place32 = y * 8 + z * 2 + c
    for n in range(1, 32):
        other = (place32 + n) % 32
        pl.semaphore_signal(
            barrier, inc=1, device_id=place(other // 8, x, (other // 2) % 4, other % 2), device_id_type=MESH
        )
    for n in range(1, 4):
        pl.semaphore_signal(barrier, inc=1, device_id=place(y, x + n, z, c), device_id_type=MESH)

    loads[0].wait()
    key0, key1 = key_ref[0], key_ref[1]
    for i in range(4):
        nodes = row * ROWS + i * BLK + lax.broadcasted_iota(jnp.int32, (BLK, FEAT), 0)
        feats = lax.broadcasted_iota(jnp.int32, (BLK, FEAT), 1)
        at = pl.ds(i * BLK, BLK)
        kept = keep_mask(nodes, feats, key0, key1)
        own[at, :] = jnp.where(kept, feat[at, :].astype(F32), 0.0).astype(BF16)
    cols[...] = col_ref[...]
    rdeg[0] = row_ref[...]
    pl.semaphore_wait(barrier, 34)

    same = yh * 4
    lead = ((yh + c) % 2) * 4
    rest = 4 - lead
    x1, x2, xo = (x + 1 + 2 * c) % 4, (x + 3 + 2 * c) % 4, (x + 2) % 4
    dev1, dev2 = place(y, x1, z, c), place(y, x2, z, c)
    pair = place(y, x, z + 1 + 2 * c, 1 - c)
    step = ROWS // CHUNKS

    def piece(panel, k):
        return xs.at[panel, pl.ds(k * step, step)]

    def own_piece(k):
        return own.at[pl.ds(k * step, step)]

    chunks = range(CHUNKS)
    first = lead + x
    last = rest + x
    across = place(y + 2, x, z, c)
    to_y = jnp.where(c == 0, y, 3 - y)
    to_z = z + jnp.where(c == 0, q, 3 - 2 * yl)
    got = [
        send(own_piece(k), piece(same + x, k), s1_s.at[0, k], s1_r.at[0, k], place(to_y, x, to_z, c), q != 0)
        for k in chunks
    ]

    d1 = [
        send(cols, deg1.at[n - 1], d1_s.at[n - 1], d1_r.at[n - 1], place(y, x + n, z, c))
        for n in range(1, 4)
    ]
    rd = [
        send(rdeg.at[0], rdeg.at[n], rd_s.at[n - 1], rd_r.at[n - 1], (row, (q + n) % 4))
        for n in range(1, 4)
    ]

    @pl.when(q == 0)
    def _():
        xs[same + x] = own[...]

    loads[1].wait()

    @pl.when(q == 0)
    def _():
        eye = lax.broadcasted_iota(jnp.int32, (BLK, BLK), 0) == lax.broadcasted_iota(jnp.int32, (BLK, BLK), 1)
        eye = jnp.where(eye, 1.0, 0.0)
        for i in range(4):
            at = pl.ds(i * BLK, BLK), pl.ds(pl.multiple_of(first * ROWS + i * BLK, BLK), BLK)
            d[at] = (d[at].astype(F32) + eye).astype(BF16)

    def wait_when(copy, when):
        pl.when(when)(copy.wait_recv)

    by1, by2, got_rest = [[], []], [], []
    for k in chunks:
        wait_when(got[k], q != 0)
        src = piece(first, k)
        by2.append(send(src, src, x_s.at[2, k], x_r.at[2, k], dev2))
        by1[0].append(send(src, src, x_s.at[0, k], x_r.at[0, k], dev1))
        got_rest.append(send(src, src, s1_s.at[1, k], s1_r.at[1, k], across))

    for copy in d1:
        copy.wait_recv()
    deg2[0] = cols[...] + deg1[0] + deg1[1] + deg1[2]
    d2 = []
    for n in range(1, 8):
        o = (me8 + n) % 8
        o_q = o % 4
        to = place((o // 4) * 2 + o_q // 2, x, zp + o_q, o_q % 2)
        d2.append(send(deg2.at[0], deg2.at[n], d2_s.at[n - 1], d2_r.at[n - 1], to))

    onward, cross = [], [[], []]
    for k in chunks:
        by2[k].wait_recv()
        src = piece(lead + x1, k)
        onward.append(send(src, src, x_s.at[3, k], x_r.at[3, k], dev2))
    for k in chunks:
        by1[0][k].wait_recv()
        src = piece(lead + x2, k)
        cross[0].append(send(src, src, z_s.at[0, k], z_r.at[0, k], pair))
    for k in chunks:
        got_rest[k].wait_recv()
        src = piece(last, k)
        by1[1].append(send(src, src, x_s.at[1, k], x_r.at[1, k], dev1))

    for copy in rd:
        copy.wait_recv()
    by_rep = [rdeg[(q + 4 - s) % 4] for s in range(4)]
    row_scale = lax.rsqrt(1.0 + ((by_rep[0] + by_rep[1]) + (by_rep[2] + by_rep[3])))
    row_cols = jnp.concatenate([row_scale, row_scale], axis=0).T
    for i in range(4):
        rsc[i] = row_cols[:, i : i + 1]
    for copy in d2:
        copy.wait_recv()
    total = deg2[0]
    for n in range(1, 8):
        total = total + deg2[n]
    scales[...] = lax.rsqrt(1.0 + total)

    narrow = scales[...].astype(BF16)

    def scale_panel(p):
        for l in range(4 * p, 4 * p + 4):
            at = pl.ds(l * BLK, BLK)
            d[:, at] = d[:, at] * narrow[l : l + 1, :]

    for k in chunks:
        for p in range(8 * k // CHUNKS, 8 * (k + 1) // CHUNKS):
            scale_panel(p)
        onward[k].wait_recv()
        src = piece(lead + xo, k)
        cross[1].append(send(src, src, z_s.at[1, k], z_r.at[1, k], pair))

    def panel_cols(p):
        return pl.ds(pl.multiple_of(p * ROWS, ROWS), ROWS)

    def term(p):
        return jnp.dot(d[:, panel_cols(p)], xs[p], preferred_element_type=F32)

    lead4 = pl.ds(pl.multiple_of(lead * ROWS, ROWS), 4 * ROWS)
    acc = jnp.dot(d[:, lead4], xs[pl.ds(lead, 4)].reshape(4 * ROWS, FEAT), preferred_element_type=F32)
    acc = acc + term(last)
    for k in chunks:
        cross[0][k].wait_recv()
    acc = acc + term(rest + x1)
    for k in chunks:
        by1[1][k].wait_recv()
    acc = acc + term(rest + x2)
    for k in chunks:
        cross[1][k].wait_recv()
    acc = acc + term(rest + xo)
    hs[...] = acc.astype(BF16)
    loads[2].wait()

    half = ROWS // 2
    partner = place(y, x, z, 1 - c)
    chip = (row, (1 - yl) * 2 + c)

    def rows128(b):
        return pl.ds(pl.multiple_of(b * BLK, BLK), BLK)

    def project(b):
        part[rows128(b), :] = (
            jnp.dot(hs[rows128(b), :], w[...], preferred_element_type=F32) * 1.25
        ).astype(BF16)

    ec = [[], [], []]
    for b in range(2):
        project((1 - c) * 2 + b)
        ec[0].append(send(part.at[rows128((1 - c) * 2 + b)], e1.at[b], e_s.at[0, b], e_r.at[0, b], partner))
    project(c * 2)
    project(c * 2 + 1)
    for b in range(2):
        ec[0][b].wait_recv()
        e2s[b] = (part[rows128(c * 2 + b), :].astype(F32) + e1[b].astype(F32)).astype(BF16)
        ec[1].append(send(e2s.at[b], e2r.at[b], e_s.at[1, b], e_r.at[1, b], chip))
    hT[...] = acc.T.astype(BF16)
    loads[3].wait()

    def activate(i):
        at = rows128(i)
        r = rsc[i]
        pre = tot[at, :].astype(F32) * r
        s = 1.0 / (1.0 + jnp.exp(-pre))
        hid[at, :] = (pre * s).astype(BF16)
        grad = cot[at, :].astype(F32) * s * (1.0 + pre * (1.0 - s)) * r
        pushed[at, :] = grad.astype(BF16)
        pushT[:, at] = grad.T.astype(BF16)

    for b in range(2):
        ec[1][b].wait_recv()
        at = rows128(c * 2 + b)
        tot[at, :] = (e2s[b].astype(F32) + e2r[b].astype(F32)).astype(BF16)
        ec[2].append(send(tot.at[at], tot.at[at], e_s.at[2, b], e_r.at[2, b], partner))
    activate(c * 2)
    activate(c * 2 + 1)
    for b in range(2):
        ec[2][b].wait_recv()
        activate((1 - c) * 2 + b)
    hid_out = pltpu.make_async_copy(hid, hid_hbm, out_sem.at[0])
    hid_out.start()

    g[...] = (jnp.dot(hT[...], pushed[...], preferred_element_type=F32) * 1.25).astype(BF16)
    place8 = y * 2 + c
    at32 = pl.ds(pl.multiple_of(place8 * 32, 32), 32)
    w1c = []
    for n in range(1, 8):
        o = (place8 + n) % 8
        src = g.at[pl.ds(pl.multiple_of(o * 32, 32), 32)]
        w1c.append(send(src, w1.at[n - 1], w1_s.at[n - 1], w1_r.at[n - 1], place(o // 2, x, z, o % 2)))

    def back(p):
        out = jnp.dot(pushT[...], d[:, panel_cols(p)], preferred_element_type=F32).astype(BF16)
        for j in range(4):
            tt[p, j] = out[:, j * BLK : (j + 1) * BLK]

    def add(*blocks):
        out = blocks[0].astype(F32)
        for block in blocks[1:]:
            out = out + block.astype(F32)
        return out.astype(BF16)

    blocks4 = range(4)
    zc, sidec, farc, nearc = [[], []], [[], []], [], []
    back(rest + xo)
    for j in blocks4:
        zc[0].append(send(tt.at[rest + xo, j], zb.at[0, j], zb_s.at[0, j], zb_r.at[0, j], pair))
    back(rest + x1)
    for j in blocks4:
        zc[1].append(send(tt.at[rest + x1, j], zb.at[1, j], zb_s.at[1, j], zb_r.at[1, j], pair))
    back(rest + x2)
    for j in blocks4:
        sidec[1].append(send(tt.at[rest + x2, j], bside.at[1, j], b_s.at[1, j], b_r.at[1, j], dev2))
    for copy in w1c:
        copy.wait_recv()
    w2[x] = add(g[at32, :], *[w1[n] for n in range(7)])
    w2c = [
        send(w2.at[x], w2.at[x], w2_s.at[n - 1], w2_r.at[n - 1], place(y, x + n, z, c)) for n in range(1, 4)
    ]

    back(last)
    back(lead + xo)
    for j in blocks4:
        zc[0][j].wait_recv()
        tt[lead + xo, j] = add(tt[lead + xo, j], zb[0, j])
        farc.append(send(tt.at[lead + xo, j], bfar.at[j], b_s.at[2, j], b_r.at[2, j], dev1))
    back(lead + x2)
    for j in blocks4:
        zc[1][j].wait_recv()
        tt[lead + x2, j] = add(tt[lead + x2, j], zb[1, j])
        sidec[0].append(send(tt.at[lead + x2, j], bside.at[0, j], b_s.at[0, j], b_r.at[0, j], dev2))

    for copy in w2c:
        copy.wait_recv()
    w3[z] = add(w2[0], w2[1], w2[2], w2[3])
    w3c = [
        send(w3.at[z], w3.at[z], w3_s.at[n - 1], w3_r.at[n - 1], place(y, x, z + n, c)) for n in range(1, 4)
    ]

    ypc = []
    for j in blocks4:
        sidec[1][j].wait_recv()
        u[1, j] = add(tt[last, j], bside[1, j])
        ypc.append(send(u.at[1, j], yp.at[j], yp_s.at[j], yp_r.at[j], across))

    back(lead + x1)
    for j in blocks4:
        farc[j].wait_recv()
        tt[lead + x1, j] = add(tt[lead + x1, j], bfar[j])
        nearc.append(send(tt.at[lead + x1, j], bnear.at[j], b_s.at[3, j], b_r.at[3, j], dev1))
    back(first)

    for copy in w3c:
        copy.wait_recv()
    g4[at32, :] = add(w3[0], w3[1], w3[2], w3[3])
    w4c = []
    for n in range(1, 8):
        o = (place8 + n) % 8
        src = g4.at[at32]
        w4c.append(send(src, src, w4_s.at[n - 1], w4_r.at[n - 1], place(o // 2, x, z, o % 2)))

    half_of = (yh + c) % 2
    for j in blocks4:
        sidec[0][j].wait_recv()
        nearc[j].wait_recv()
        ypc[j].wait_recv()
        u[0, j] = add(tt[first, j], bside[0, j], bnear[j], yp[j])
        to = place(2 * half_of + j // 2, x, zp, j % 2)
        send(u.at[0, j], fin.at[q], f_s.at[j], f_r.at[q], to, q != 0 if j == 0 else None)

    @pl.when(q == 0)
    def _():
        fin[0] = u[0, 0]

    for n in range(4):
        copy = remote(u.at[0, 0], fin.at[n], f_s.at[0], f_r.at[n], (row, q))
        if n == 0:
            wait_when(copy, q != 0)
        else:
            copy.wait_recv()
    proj = fin[0].astype(F32)
    for n in range(1, 4):
        proj = proj + fin[n].astype(F32)
    fg[...] = proj.T.astype(BF16)
    fg_out = pltpu.make_async_copy(fg, fg_hbm, out_sem.at[1])
    fg_out.start()
    for copy in w4c:
        copy.wait_recv()
    wg_out = pltpu.make_async_copy(g4, wg_hbm, out_sem.at[2])
    wg_out.start()
    for copy, when in sent:
        if when is None:
            copy.wait_send()
        else:
            pl.when(when)(copy.wait_send)
    hid_out.wait()
    fg_out.wait()
    wg_out.wait()


def layer(drop_key, features, weight, d, col, row, cotangent):
    dma = pltpu.SemaphoreType.DMA
    vmem = pltpu.VMEM
    any_spec = pl.BlockSpec(memory_space=pl.ANY)
    vmem_spec = pl.BlockSpec(memory_space=pltpu.VMEM)
    return pl.pallas_call(
        layer_kernel,
        out_shape=[
            jax.ShapeDtypeStruct((ROWS, FEAT), BF16),
            jax.ShapeDtypeStruct((FEAT, FEAT), BF16),
            jax.ShapeDtypeStruct((BLK, FEAT), BF16),
        ],
        in_specs=[
            pl.BlockSpec(memory_space=pltpu.SMEM),
            any_spec, any_spec, any_spec, vmem_spec, vmem_spec, any_spec,
        ],
        out_specs=[any_spec, any_spec, any_spec],
        scratch_shapes=[
            vmem((ROWS, FEAT), BF16),
            vmem((FEAT, FEAT), BF16),
            vmem((ROWS, 32 * BLK), BF16),
            vmem((ROWS, FEAT), BF16),
            vmem((ROWS, FEAT), BF16),
            vmem((8, ROWS, FEAT), BF16),
            vmem((32, BLK), F32),
            vmem((32, BLK), F32),
            vmem((3, 32, BLK), F32),
            vmem((8, 32, BLK), F32),
            vmem((4, 4, BLK), F32),
            vmem((4, BLK, 1), F32),
            vmem((ROWS, FEAT), BF16),
            vmem((FEAT, ROWS), BF16),
            vmem((ROWS, FEAT), BF16),
            vmem((2, BLK, FEAT), BF16),
            vmem((2, BLK, FEAT), BF16),
            vmem((2, BLK, FEAT), BF16),
            vmem((ROWS, FEAT), BF16),
            vmem((ROWS, FEAT), BF16),
            vmem((ROWS, FEAT), BF16),
            vmem((FEAT, ROWS), BF16),
            vmem((8, 4, FEAT, BLK), BF16),
            vmem((2, 4, FEAT, BLK), BF16),
            vmem((4, FEAT, BLK), BF16),
            vmem((4, FEAT, BLK), BF16),
            vmem((2, 4, FEAT, BLK), BF16),
            vmem((2, 4, FEAT, BLK), BF16),
            vmem((4, FEAT, BLK), BF16),
            vmem((4, FEAT, BLK), BF16),
            vmem((FEAT, FEAT), BF16),
            vmem((7, 32, FEAT), BF16),
            vmem((4, 32, FEAT), BF16),
            vmem((4, 32, FEAT), BF16),
            vmem((FEAT, FEAT), BF16),
            vmem((BLK, FEAT), BF16),
            dma((4,)), dma((3,)),
            dma((2, CHUNKS)), dma((2, CHUNKS)),
            dma((4, CHUNKS)), dma((4, CHUNKS)),
            dma((2, CHUNKS)), dma((2, CHUNKS)),
            dma((3,)), dma((3,)), dma((7,)), dma((7,)), dma((3,)), dma((3,)),
            dma((3, 2)), dma((3, 2)),
            dma((2, 4)), dma((2, 4)), dma((4, 4)), dma((4, 4)),
            dma((4,)), dma((4,)), dma((4,)), dma((4,)),
            dma((7,)), dma((7,)), dma((3,)), dma((3,)), dma((3,)), dma((3,)),
            dma((7,)), dma((7,)),
        ],
        compiler_params=pltpu.CompilerParams(
            collective_id=0, has_side_effects=True, vmem_limit_bytes=24 << 20
        ),
        name="layer",
    )(drop_key, features, weight, d, col, row, cotangent)


def finish_kernel(key_ref, hid_ref, g_ref, proj_ref, w_ref, hid_out, wg_out, fg_out):
    hid_out[...] = hid_ref[...]
    wg_out[...] = g_ref[...].astype(F32)
    back_proj = (
        lax.dot_general(proj_ref[...], w_ref[...], (((1,), (1,)), ((), ())), preferred_element_type=F32) * 1.25
    )
    first = lax.axis_index("row") * ROWS + lax.axis_index("rep") * BLK
    nodes = first + lax.broadcasted_iota(jnp.int32, (BLK, FEAT), 0)
    feats = lax.broadcasted_iota(jnp.int32, (BLK, FEAT), 1)
    kept = keep_mask(nodes, feats, key_ref[0], key_ref[1])
    fg_out[...] = jnp.where(kept, back_proj, 0.0).astype(BF16)


def finish(drop_key, hid, g, proj, weight):
    return pl.pallas_call(
        finish_kernel,
        out_shape=[
            jax.ShapeDtypeStruct((ROWS, FEAT), BF16),
            jax.ShapeDtypeStruct((FEAT, FEAT), F32),
            jax.ShapeDtypeStruct((BLK, FEAT), BF16),
        ],
        in_specs=[pl.BlockSpec(memory_space=pltpu.SMEM)] + [pl.BlockSpec(memory_space=pltpu.VMEM)] * 4,
        out_specs=[pl.BlockSpec(memory_space=pltpu.VMEM)] * 3,
        compiler_params=pltpu.CompilerParams(vmem_limit_bytes=4 << 20),
        name="finish",
    )(drop_key, hid, g, proj, weight)


def shards(features, weight, adj_tiles, block_cols, edge_keep, drop_key, cotangent):
    features, weight, adj_tiles, block_cols, edge_keep, drop_key, cotangent = (
        pltpu.with_memory_space_constraint(a, pltpu.HBM)
        for a in (features, weight, adj_tiles, block_cols, edge_keep, drop_key, cotangent)
    )
    d, col, row = build(block_cols, edge_keep, adj_tiles)
    hidden, grad, proj = layer(drop_key, features, weight, d, col, row, cotangent)
    return finish(drop_key, hidden, grad, proj, weight)


def solution(mesh):
    in_specs = (
        P("row", None),
        P(),
        P("row", "rep", None, None),
        P("row", "rep"),
        P("row", "rep"),
        P(),
        P("row", None),
    )
    out_specs = (P("row", None), P(), P(("row", "rep"), None))
    return jax.shard_map(shards, mesh=mesh, in_specs=in_specs, out_specs=out_specs, check_vma=False)
```

```python
import functools

import jax
import jax.numpy as jnp
from jax import lax
from jax.experimental import pallas as pl
from jax.experimental.pallas import tpu as pltpu
from jax.sharding import PartitionSpec as P

MESH = pl.DeviceIdType.MESH
BLK = 128
FEAT = 256
ROWS = 512
CHUNKS = 4
F32 = jnp.float32
BF16 = jnp.bfloat16


def keep_mask(node_ids, feat_ids, key0, key1):
    mixed = node_ids * 73856093 ^ feat_ids * 19349663 ^ key0 * 83492791 ^ key1
    mixed = mixed ^ lax.shift_right_logical(mixed, jnp.int32(13))
    mixed = mixed * 1274126177
    mixed = mixed ^ lax.shift_right_logical(mixed, jnp.int32(16))
    return mixed & 1023 < 819


def place(y, x, z, c):
    y, x, z = y % 4, x % 4, z % 4
    return ((y // 2) * 16 + x * 4 + z, (y % 2) * 2 + c)


def build_kernel(
    key_ref, blk_ref, keep_ref, feat_hbm, tiles_hbm, own_ref, gate_ref, d_ref, col_ref, row_ref, feat, tiles, sem
):
    loads = [pltpu.make_async_copy(tiles_hbm.at[i], tiles.at[i], sem.at[i]) for i in range(4)]
    loads.append(pltpu.make_async_copy(feat_hbm, feat, sem.at[4]))
    loads[4].start()
    for copy in loads[:4]:
        copy.start()
    col_ref[...] = jnp.zeros_like(col_ref)
    d_ref[...] = jnp.zeros_like(d_ref)

    first_node = lax.axis_index("row") * ROWS

    def kept(start):
        nodes = first_node + start + lax.broadcasted_iota(jnp.int32, (BLK, FEAT), 0)
        feats = lax.broadcasted_iota(jnp.int32, (BLK, FEAT), 1)
        return keep_mask(nodes, feats, key_ref[0], key_ref[1])

    gate_ref[...] = jnp.where(kept(lax.axis_index("rep") * BLK), 1.0, 0.0)
    loads[4].wait()
    for i in range(4):
        at = pl.ds(i * BLK, BLK)
        own_ref[at, :] = jnp.where(kept(i * BLK), feat[at, :].astype(F32), 0.0).astype(BF16)
    for i in range(4):
        loads[i].wait()
        rows = pl.ds(i * BLK, BLK)
        row_acc = jnp.zeros((BLK, BLK), F32)
        for k in range(16):
            col = blk_ref[i, k]
            slot = (col >> 4) * 4 + (col & 3)
            tile = tiles[i, k] * keep_ref[i, k].astype(BF16)
            at = pl.ds(pl.multiple_of(slot * BLK, BLK), BLK)
            d_ref[rows, at] = d_ref[rows, at] + tile
            wide = tile.astype(F32)
            col_ref[pl.ds(slot, 1), :] += jnp.sum(wide, axis=0, keepdims=True)
            row_acc = row_acc + wide
        row_ref[pl.ds(i, 1), :] = jnp.sum(row_acc.T, axis=0, keepdims=True)


def build(drop_key, cols, keep, features, tiles):
    smem, vmem = pl.BlockSpec(memory_space=pltpu.SMEM), pl.BlockSpec(memory_space=pltpu.VMEM)
    any_spec = pl.BlockSpec(memory_space=pl.ANY)
    return pl.pallas_call(
        build_kernel,
        in_specs=[smem, smem, smem, any_spec, any_spec],
        out_specs=[vmem] * 5,
        out_shape=[
            jax.ShapeDtypeStruct((ROWS, FEAT), BF16),
            jax.ShapeDtypeStruct((BLK, FEAT), F32),
            jax.ShapeDtypeStruct((ROWS, 32 * BLK), BF16),
            jax.ShapeDtypeStruct((32, BLK), F32),
            jax.ShapeDtypeStruct((4, BLK), F32),
        ],
        scratch_shapes=[
            pltpu.VMEM((ROWS, FEAT), BF16),
            pltpu.VMEM((4, 16, BLK, BLK), BF16),
            pltpu.SemaphoreType.DMA((5,)),
        ],
        compiler_params=pltpu.CompilerParams(vmem_limit_bytes=12 << 20),
        name="build",
    )(drop_key, cols, keep, features, tiles)


def layer_kernel(
    own, w_hbm, d_hbm, col_ref, row_ref, cot_hbm,
    hid, wg_ref, proj_ref, w,
    d, cot, xs, cols, scales, deg1, deg2, rdeg, rsc, hs, hT, part, e1, e2s, e2r, tot,
    pushed, pushT, tt, zb, bfar, bnear, bside, u, yp, fin, g, w1, w2, w3, g4,
    in_sem, s1_s, s1_r, x_s, x_r, z_s, z_r, d1_s, d1_r, d2_s, d2_r, rd_s, rd_r,
    e_s, e_r, zb_s, zb_r, b_s, b_r, yp_s, yp_r, f_s, f_r,
    w1_s, w1_r, w2_s, w2_r, w3_s, w3_r, w4_s, w4_r,
):
    row = lax.axis_index("row")
    q = lax.axis_index("rep")
    y = (row // 16) * 2 + q // 2
    x = (row // 4) % 4
    z = row % 4
    c = q % 2
    yh = row // 16
    yl = q // 2
    zp = z + 4 - q
    me8 = yh * 4 + q
    sent = []

    def remote(src, dst, ssem, rsem, to):
        return pltpu.make_async_remote_copy(
            src_ref=src, dst_ref=dst, send_sem=ssem, recv_sem=rsem, device_id=to, device_id_type=MESH
        )

    def send(src, dst, ssem, rsem, to, when=None):
        copy = remote(src, dst, ssem, rsem, to)
        if when is None:
            copy.start()
        else:
            pl.when(when)(copy.start)
        sent.append((copy, when))
        return copy

    loads = [
        pltpu.make_async_copy(src, dst, in_sem.at[n])
        for n, (src, dst) in enumerate(((d_hbm, d), (w_hbm, w), (cot_hbm, cot)))
    ]
    for copy in loads:
        copy.start()

    barrier = pltpu.get_barrier_semaphore()
    place32 = y * 8 + z * 2 + c
    for n in range(1, 32):
        other = (place32 + n) % 32
        pl.semaphore_signal(
            barrier, inc=1, device_id=place(other // 8, x, (other // 2) % 4, other % 2), device_id_type=MESH
        )
    for n in range(1, 4):
        pl.semaphore_signal(barrier, inc=1, device_id=place(y, x + n, z, c), device_id_type=MESH)

    cols[...] = col_ref[...]
    rdeg[0] = row_ref[...]
    pl.semaphore_wait(barrier, 34)

    same = yh * 4
    lead = ((yh + c) % 2) * 4
    rest = 4 - lead
    x1, x2, xo = (x + 1 + 2 * c) % 4, (x + 3 + 2 * c) % 4, (x + 2) % 4
    dev1, dev2 = place(y, x1, z, c), place(y, x2, z, c)
    pair = place(y, x, z + 1 + 2 * c, 1 - c)
    step = ROWS // CHUNKS

    def piece(panel, k):
        return xs.at[panel, pl.ds(k * step, step)]

    def own_piece(k):
        return own.at[pl.ds(k * step, step)]

    chunks = range(CHUNKS)
    first = lead + x
    last = rest + x
    across = place(y + 2, x, z, c)
    to_y = jnp.where(c == 0, y, 3 - y)
    to_z = z + jnp.where(c == 0, q, 3 - 2 * yl)
    got = [
        send(own_piece(k), piece(same + x, k), s1_s.at[0, k], s1_r.at[0, k], place(to_y, x, to_z, c), q != 0)
        for k in chunks
    ]

    d1 = [
        send(cols, deg1.at[n - 1], d1_s.at[n - 1], d1_r.at[n - 1], place(y, x + n, z, c))
        for n in range(1, 4)
    ]
    rd = [
        send(rdeg.at[0], rdeg.at[n], rd_s.at[n - 1], rd_r.at[n - 1], (row, (q + n) % 4))
        for n in range(1, 4)
    ]

    @pl.when(q == 0)
    def _():
        xs[same + x] = own[...]

    loads[0].wait()

    @pl.when(q == 0)
    def _():
        eye = lax.broadcasted_iota(jnp.int32, (BLK, BLK), 0) == lax.broadcasted_iota(jnp.int32, (BLK, BLK), 1)
        eye = jnp.where(eye, 1.0, 0.0)
        for i in range(4):
            at = pl.ds(i * BLK, BLK), pl.ds(pl.multiple_of(first * ROWS + i * BLK, BLK), BLK)
            d[at] = (d[at].astype(F32) + eye).astype(BF16)

    def drain():
        for copy, when in sent:
            if when is None:
                copy.wait_send()
            else:
                pl.when(when)(copy.wait_send)
        sent.clear()

    def wait_when(copy, when):
        pl.when(when)(copy.wait_recv)

    by1, by2, got_rest = [[], []], [], []
    for k in chunks:
        wait_when(got[k], q != 0)
        src = piece(first, k)
        by2.append(send(src, src, x_s.at[2, k], x_r.at[2, k], dev2))
        by1[0].append(send(src, src, x_s.at[0, k], x_r.at[0, k], dev1))
        got_rest.append(send(src, src, s1_s.at[1, k], s1_r.at[1, k], across))

    for copy in d1:
        copy.wait_recv()
    deg2[0] = cols[...] + deg1[0] + deg1[1] + deg1[2]
    d2 = []
    for n in range(1, 8):
        o = (me8 + n) % 8
        o_q = o % 4
        to = place((o // 4) * 2 + o_q // 2, x, zp + o_q, o_q % 2)
        d2.append(send(deg2.at[0], deg2.at[n], d2_s.at[n - 1], d2_r.at[n - 1], to))

    onward, cross = [], [[], []]
    for k in chunks:
        by2[k].wait_recv()
        src = piece(lead + x1, k)
        onward.append(send(src, src, x_s.at[3, k], x_r.at[3, k], dev2))
    for k in chunks:
        by1[0][k].wait_recv()
        src = piece(lead + x2, k)
        cross[0].append(send(src, src, z_s.at[0, k], z_r.at[0, k], pair))
    for k in chunks:
        got_rest[k].wait_recv()
        src = piece(last, k)
        by1[1].append(send(src, src, x_s.at[1, k], x_r.at[1, k], dev1))

    for copy in rd:
        copy.wait_recv()
    by_rep = [rdeg[(q + 4 - s) % 4] for s in range(4)]
    row_scale = lax.rsqrt(1.0 + ((by_rep[0] + by_rep[1]) + (by_rep[2] + by_rep[3])))
    row_cols = jnp.concatenate([row_scale, row_scale], axis=0).T
    for i in range(4):
        rsc[i] = row_cols[:, i : i + 1]
    for copy in d2:
        copy.wait_recv()
    total = deg2[0]
    for n in range(1, 8):
        total = total + deg2[n]
    scales[...] = lax.rsqrt(1.0 + total)

    narrow = scales[...].astype(BF16)

    def scale_panel(p):
        for l in range(4 * p, 4 * p + 4):
            at = pl.ds(l * BLK, BLK)
            d[:, at] = d[:, at] * narrow[l : l + 1, :]

    for k in chunks:
        for p in range(8 * k // CHUNKS, 8 * (k + 1) // CHUNKS):
            scale_panel(p)
        onward[k].wait_recv()
        src = piece(lead + xo, k)
        cross[1].append(send(src, src, z_s.at[1, k], z_r.at[1, k], pair))

    def panel_cols(p):
        return pl.ds(pl.multiple_of(p * ROWS, ROWS), ROWS)

    def term(p):
        return jnp.dot(d[:, panel_cols(p)], xs[p], preferred_element_type=F32)

    lead4 = pl.ds(pl.multiple_of(lead * ROWS, ROWS), 4 * ROWS)
    acc = jnp.dot(d[:, lead4], xs[pl.ds(lead, 4)].reshape(4 * ROWS, FEAT), preferred_element_type=F32)
    acc = acc + term(last)
    for k in chunks:
        cross[0][k].wait_recv()
    acc = acc + term(rest + x1)
    for k in chunks:
        by1[1][k].wait_recv()
    acc = acc + term(rest + x2)
    for k in chunks:
        cross[1][k].wait_recv()
    acc = acc + term(rest + xo)
    hs[...] = acc.astype(BF16)
    loads[1].wait()

    half = ROWS // 2
    partner = place(y, x, z, 1 - c)
    chip = (row, (1 - yl) * 2 + c)

    def rows128(b):
        return pl.ds(pl.multiple_of(b * BLK, BLK), BLK)

    def project(b):
        part[rows128(b), :] = (
            jnp.dot(hs[rows128(b), :], w[...], preferred_element_type=F32) * 1.25
        ).astype(BF16)

    ec = [[], [], []]
    for b in range(2):
        project((1 - c) * 2 + b)
        ec[0].append(send(part.at[rows128((1 - c) * 2 + b)], e1.at[b], e_s.at[0, b], e_r.at[0, b], partner))
    project(c * 2)
    project(c * 2 + 1)
    for b in range(2):
        ec[0][b].wait_recv()
        e2s[b] = (part[rows128(c * 2 + b), :].astype(F32) + e1[b].astype(F32)).astype(BF16)
        ec[1].append(send(e2s.at[b], e2r.at[b], e_s.at[1, b], e_r.at[1, b], chip))
    e_sent = sent[-4:]
    del sent[-4:]
    drain()
    sent.extend(e_sent)
    hT[...] = acc.T.astype(BF16)
    loads[2].wait()

    def activate(i):
        at = rows128(i)
        r = rsc[i]
        pre = tot[at, :].astype(F32) * r
        s = 1.0 / (1.0 + jnp.exp(-pre))
        hid[at, :] = (pre * s).astype(BF16)
        grad = cot[at, :].astype(F32) * s * (1.0 + pre * (1.0 - s)) * r
        pushed[at, :] = grad.astype(BF16)
        pushT[:, at] = grad.T.astype(BF16)

    for b in range(2):
        ec[1][b].wait_recv()
        at = rows128(c * 2 + b)
        tot[at, :] = (e2s[b].astype(F32) + e2r[b].astype(F32)).astype(BF16)
        ec[2].append(send(tot.at[at], tot.at[at], e_s.at[2, b], e_r.at[2, b], partner))
    activate(c * 2)
    activate(c * 2 + 1)
    for b in range(2):
        ec[2][b].wait_recv()
        activate((1 - c) * 2 + b)

    g[...] = (jnp.dot(hT[...], pushed[...], preferred_element_type=F32) * 1.25).astype(BF16)
    place8 = y * 2 + c
    at32 = pl.ds(pl.multiple_of(place8 * 32, 32), 32)
    w1c = []
    for n in range(1, 8):
        o = (place8 + n) % 8
        src = g.at[pl.ds(pl.multiple_of(o * 32, 32), 32)]
        w1c.append(send(src, w1.at[n - 1], w1_s.at[n - 1], w1_r.at[n - 1], place(o // 2, x, z, o % 2)))

    def back(p):
        out = jnp.dot(pushT[...], d[:, panel_cols(p)], preferred_element_type=F32).astype(BF16)
        for j in range(4):
            tt[p, j] = out[:, j * BLK : (j + 1) * BLK]

    def add(*blocks):
        out = blocks[0].astype(F32)
        for block in blocks[1:]:
            out = out + block.astype(F32)
        return out.astype(BF16)

    blocks4 = range(4)
    zc, sidec, farc, nearc = [[], []], [[], []], [], []
    back(rest + xo)
    for j in blocks4:
        zc[0].append(send(tt.at[rest + xo, j], zb.at[0, j], zb_s.at[0, j], zb_r.at[0, j], pair))
    back(rest + x1)
    for j in blocks4:
        zc[1].append(send(tt.at[rest + x1, j], zb.at[1, j], zb_s.at[1, j], zb_r.at[1, j], pair))
    back(rest + x2)
    for j in blocks4:
        sidec[1].append(send(tt.at[rest + x2, j], bside.at[1, j], b_s.at[1, j], b_r.at[1, j], dev2))
    for copy in w1c:
        copy.wait_recv()
    w2[x] = add(g[at32, :], *[w1[n] for n in range(7)])
    w2c = [
        send(w2.at[x], w2.at[x], w2_s.at[n - 1], w2_r.at[n - 1], place(y, x + n, z, c)) for n in range(1, 4)
    ]

    back(last)
    back(lead + xo)
    for j in blocks4:
        zc[0][j].wait_recv()
        tt[lead + xo, j] = add(tt[lead + xo, j], zb[0, j])
        farc.append(send(tt.at[lead + xo, j], bfar.at[j], b_s.at[2, j], b_r.at[2, j], dev1))
    ypc = []
    for j in blocks4:
        sidec[1][j].wait_recv()
        u[1, j] = add(tt[last, j], bside[1, j])
        ypc.append(send(u.at[1, j], yp.at[j], yp_s.at[j], yp_r.at[j], across))

    back(lead + x2)
    for j in blocks4:
        zc[1][j].wait_recv()
        tt[lead + x2, j] = add(tt[lead + x2, j], zb[1, j])
        sidec[0].append(send(tt.at[lead + x2, j], bside.at[0, j], b_s.at[0, j], b_r.at[0, j], dev2))

    for copy in w2c:
        copy.wait_recv()
    w3[z] = add(w2[0], w2[1], w2[2], w2[3])
    w3c = [
        send(w3.at[z], w3.at[z], w3_s.at[n - 1], w3_r.at[n - 1], place(y, x, z + n, c)) for n in range(1, 4)
    ]

    back(lead + x1)
    for j in blocks4:
        farc[j].wait_recv()
        tt[lead + x1, j] = add(tt[lead + x1, j], bfar[j])
        nearc.append(send(tt.at[lead + x1, j], bnear.at[j], b_s.at[3, j], b_r.at[3, j], dev1))
    back(first)

    for copy in w3c:
        copy.wait_recv()
    g4[at32, :] = add(w3[0], w3[1], w3[2], w3[3])
    w4c = []
    for n in range(1, 8):
        o = (place8 + n) % 8
        src = g4.at[at32]
        w4c.append(send(src, src, w4_s.at[n - 1], w4_r.at[n - 1], place(o // 2, x, z, o % 2)))

    half_of = (yh + c) % 2
    for j in blocks4:
        sidec[0][j].wait_recv()
        nearc[j].wait_recv()
        ypc[j].wait_recv()
        u[0, j] = add(tt[first, j], bside[0, j], bnear[j], yp[j])
        to = place(2 * half_of + j // 2, x, zp, j % 2)
        send(u.at[0, j], fin.at[q], f_s.at[j], f_r.at[q], to, q != 0 if j == 0 else None)

    @pl.when(q == 0)
    def _():
        fin[0] = u[0, 0]

    for n in range(4):
        copy = remote(u.at[0, 0], fin.at[n], f_s.at[0], f_r.at[n], (row, q))
        if n == 0:
            wait_when(copy, q != 0)
        else:
            copy.wait_recv()
    proj = fin[0].astype(F32)
    for n in range(1, 4):
        proj = proj + fin[n].astype(F32)
    proj_ref[...] = proj.T.astype(BF16)
    for copy in w4c:
        copy.wait_recv()
    wg_ref[...] = g4[...]
    drain()


def layer(own, weight, d, col, row, cotangent):
    dma = pltpu.SemaphoreType.DMA
    vmem = pltpu.VMEM
    any_spec = pl.BlockSpec(memory_space=pl.ANY)
    vmem_spec = pl.BlockSpec(memory_space=pltpu.VMEM)
    return pl.pallas_call(
        layer_kernel,
        out_shape=[
            jax.ShapeDtypeStruct((ROWS, FEAT), BF16),
            jax.ShapeDtypeStruct((FEAT, FEAT), BF16),
            jax.ShapeDtypeStruct((BLK, FEAT), BF16),
            jax.ShapeDtypeStruct((FEAT, FEAT), BF16),
        ],
        in_specs=[vmem_spec, any_spec, any_spec, vmem_spec, vmem_spec, any_spec],
        out_specs=[vmem_spec] * 4,
        scratch_shapes=[
            vmem((ROWS, 32 * BLK), BF16),
            vmem((ROWS, FEAT), BF16),
            vmem((8, ROWS, FEAT), BF16),
            vmem((32, BLK), F32),
            vmem((32, BLK), F32),
            vmem((3, 32, BLK), F32),
            vmem((8, 32, BLK), F32),
            vmem((4, 4, BLK), F32),
            vmem((4, BLK, 1), F32),
            vmem((ROWS, FEAT), BF16),
            vmem((FEAT, ROWS), BF16),
            vmem((ROWS, FEAT), BF16),
            vmem((2, BLK, FEAT), BF16),
            vmem((2, BLK, FEAT), BF16),
            vmem((2, BLK, FEAT), BF16),
            vmem((ROWS, FEAT), BF16),
            vmem((ROWS, FEAT), BF16),
            vmem((FEAT, ROWS), BF16),
            vmem((8, 4, FEAT, BLK), BF16),
            vmem((2, 4, FEAT, BLK), BF16),
            vmem((4, FEAT, BLK), BF16),
            vmem((4, FEAT, BLK), BF16),
            vmem((2, 4, FEAT, BLK), BF16),
            vmem((2, 4, FEAT, BLK), BF16),
            vmem((4, FEAT, BLK), BF16),
            vmem((4, FEAT, BLK), BF16),
            vmem((FEAT, FEAT), BF16),
            vmem((7, 32, FEAT), BF16),
            vmem((4, 32, FEAT), BF16),
            vmem((4, 32, FEAT), BF16),
            vmem((FEAT, FEAT), BF16),
            dma((3,)),
            dma((2, CHUNKS)), dma((2, CHUNKS)),
            dma((4, CHUNKS)), dma((4, CHUNKS)),
            dma((2, CHUNKS)), dma((2, CHUNKS)),
            dma((3,)), dma((3,)), dma((7,)), dma((7,)), dma((3,)), dma((3,)),
            dma((3, 2)), dma((3, 2)),
            dma((2, 4)), dma((2, 4)), dma((4, 4)), dma((4, 4)),
            dma((4,)), dma((4,)), dma((4,)), dma((4,)),
            dma((7,)), dma((7,)), dma((3,)), dma((3,)), dma((3,)), dma((3,)),
            dma((7,)), dma((7,)),
        ],
        compiler_params=pltpu.CompilerParams(
            collective_id=0, has_side_effects=True, vmem_limit_bytes=24 << 20
        ),
        name="layer",
    )(own, weight, d, col, row, cotangent)


def finish_kernel(hid_ref, g_ref, proj_ref, w_ref, gate_ref, hid_out, wg_out, fg_out):
    hid_out[...] = hid_ref[...]
    wg_out[...] = g_ref[...].astype(F32)
    back_proj = (
        lax.dot_general(proj_ref[...], w_ref[...], (((1,), (1,)), ((), ())), preferred_element_type=F32) * 1.25
    )
    fg_out[...] = jnp.where(gate_ref[...] > 0.0, back_proj, 0.0).astype(BF16)


def finish(hid, g, proj, weight, gate):
    return pl.pallas_call(
        finish_kernel,
        out_shape=[
            jax.ShapeDtypeStruct((ROWS, FEAT), BF16),
            jax.ShapeDtypeStruct((FEAT, FEAT), F32),
            jax.ShapeDtypeStruct((BLK, FEAT), BF16),
        ],
        in_specs=[pl.BlockSpec(memory_space=pltpu.VMEM)] * 5,
        out_specs=[pl.BlockSpec(memory_space=pltpu.VMEM)] * 3,
        compiler_params=pltpu.CompilerParams(vmem_limit_bytes=4 << 20),
        name="finish",
    )(hid, g, proj, weight, gate)


def shards(features, weight, adj_tiles, block_cols, edge_keep, drop_key, cotangent):
    features, weight, adj_tiles, block_cols, edge_keep, drop_key, cotangent = (
        pltpu.with_memory_space_constraint(a, pltpu.HBM)
        for a in (features, weight, adj_tiles, block_cols, edge_keep, drop_key, cotangent)
    )
    own, gate, d, col, row = build(drop_key, block_cols, edge_keep, features, adj_tiles)
    hidden, grad, proj, kept_weight = layer(own, weight, d, col, row, cotangent)
    return finish(hidden, grad, proj, kept_weight, gate)


def solution(mesh):
    in_specs = (
        P("row", None),
        P(),
        P("row", "rep", None, None),
        P("row", "rep"),
        P("row", "rep"),
        P(),
        P("row", None),
    )
    out_specs = (P("row", None), P(), P(("row", "rep"), None))
    return jax.shard_map(shards, mesh=mesh, in_specs=in_specs, out_specs=out_specs, check_vma=False)
```

```python
import functools

import jax
import jax.numpy as jnp
from jax import lax
from jax.experimental import pallas as pl
from jax.experimental.pallas import tpu as pltpu
from jax.sharding import PartitionSpec as P

MESH = pl.DeviceIdType.MESH
BLK = 128
FEAT = 256
ROWS = 512
CHUNKS = 4
F32 = jnp.float32
BF16 = jnp.bfloat16


def keep_mask(node_ids, feat_ids, key0, key1):
    mixed = node_ids * 73856093 ^ feat_ids * 19349663 ^ key0 * 83492791 ^ key1
    mixed = mixed ^ lax.shift_right_logical(mixed, jnp.int32(13))
    mixed = mixed * 1274126177
    mixed = mixed ^ lax.shift_right_logical(mixed, jnp.int32(16))
    return mixed & 1023 < 819


def place(y, x, z, c):
    y, x, z = y % 4, x % 4, z % 4
    return ((y // 2) * 16 + x * 4 + z, (y % 2) * 2 + c)


def build_kernel(
    key_ref, blk_ref, keep_ref, feat_hbm, tiles_hbm, own_ref, gate_ref, d_ref, col_ref, row_ref, feat, tiles, sem
):
    loads = [pltpu.make_async_copy(tiles_hbm.at[i], tiles.at[i], sem.at[i]) for i in range(4)]
    loads.append(pltpu.make_async_copy(feat_hbm, feat, sem.at[4]))
    loads[4].start()
    for copy in loads[:4]:
        copy.start()
    col_ref[...] = jnp.zeros_like(col_ref)
    d_ref[...] = jnp.zeros_like(d_ref)

    first_node = lax.axis_index("row") * ROWS

    def kept(start):
        nodes = first_node + start + lax.broadcasted_iota(jnp.int32, (BLK, FEAT), 0)
        feats = lax.broadcasted_iota(jnp.int32, (BLK, FEAT), 1)
        return keep_mask(nodes, feats, key_ref[0], key_ref[1])

    gate_ref[...] = jnp.where(kept(lax.axis_index("rep") * BLK), 1.0, 0.0)
    loads[4].wait()
    for i in range(4):
        at = pl.ds(i * BLK, BLK)
        own_ref[at, :] = jnp.where(kept(i * BLK), feat[at, :].astype(F32), 0.0).astype(BF16)
    for i in range(4):
        loads[i].wait()
        rows = pl.ds(i * BLK, BLK)
        row_acc = jnp.zeros((BLK, BLK), F32)
        for k in range(16):
            col = blk_ref[i, k]
            slot = (col >> 4) * 4 + (col & 3)
            tile = tiles[i, k] * keep_ref[i, k].astype(BF16)
            at = pl.ds(pl.multiple_of(slot * BLK, BLK), BLK)
            d_ref[rows, at] = d_ref[rows, at] + tile
            wide = tile.astype(F32)
            col_ref[pl.ds(slot, 1), :] += jnp.sum(wide, axis=0, keepdims=True)
            row_acc = row_acc + wide
        row_ref[pl.ds(i, 1), :] = jnp.sum(row_acc.T, axis=0, keepdims=True)


def build(drop_key, cols, keep, features, tiles):
    smem, vmem = pl.BlockSpec(memory_space=pltpu.SMEM), pl.BlockSpec(memory_space=pltpu.VMEM)
    any_spec = pl.BlockSpec(memory_space=pl.ANY)
    return pl.pallas_call(
        build_kernel,
        in_specs=[smem, smem, smem, any_spec, any_spec],
        out_specs=[vmem] * 5,
        out_shape=[
            jax.ShapeDtypeStruct((ROWS, FEAT), BF16),
            jax.ShapeDtypeStruct((BLK, FEAT), F32),
            jax.ShapeDtypeStruct((ROWS, 32 * BLK), BF16),
            jax.ShapeDtypeStruct((32, BLK), F32),
            jax.ShapeDtypeStruct((4, BLK), F32),
        ],
        scratch_shapes=[
            pltpu.VMEM((ROWS, FEAT), BF16),
            pltpu.VMEM((4, 16, BLK, BLK), BF16),
            pltpu.SemaphoreType.DMA((5,)),
        ],
        compiler_params=pltpu.CompilerParams(vmem_limit_bytes=12 << 20),
        name="build",
    )(drop_key, cols, keep, features, tiles)


def layer_kernel(
    own, w_hbm, d_hbm, col_ref, row_ref, cot_hbm,
    hid, wg_ref, proj_ref, w,
    d, cot, xs, cols, scales, deg1, deg2, rdeg, rsc, hs, hT, part, e1, e2s, e2r, tot,
    pushed, pushT, tt, zb, bfar, bnear, bside, u, yp, fin, g, w1, w2, w3, g4,
    in_sem, s1_s, s1_r, x_s, x_r, z_s, z_r, d1_s, d1_r, d2_s, d2_r, rd_s, rd_r,
    e_s, e_r, zb_s, zb_r, b_s, b_r, yp_s, yp_r, f_s, f_r,
    w1_s, w1_r, w2_s, w2_r, w3_s, w3_r, w4_s, w4_r,
):
    row = lax.axis_index("row")
    q = lax.axis_index("rep")
    y = (row // 16) * 2 + q // 2
    x = (row // 4) % 4
    z = row % 4
    c = q % 2
    yh = row // 16
    yl = q // 2
    zp = z + 4 - q
    me8 = yh * 4 + q
    sent = []

    def remote(src, dst, ssem, rsem, to):
        return pltpu.make_async_remote_copy(
            src_ref=src, dst_ref=dst, send_sem=ssem, recv_sem=rsem, device_id=to, device_id_type=MESH
        )

    def send(src, dst, ssem, rsem, to, when=None):
        copy = remote(src, dst, ssem, rsem, to)
        if when is None:
            copy.start()
        else:
            pl.when(when)(copy.start)
        sent.append((copy, when))
        return copy

    loads = [
        pltpu.make_async_copy(src, dst, in_sem.at[n])
        for n, (src, dst) in enumerate(((d_hbm, d), (w_hbm, w), (cot_hbm, cot)))
    ]
    for copy in loads:
        copy.start()

    barrier = pltpu.get_barrier_semaphore()
    place32 = y * 8 + z * 2 + c
    for n in range(1, 32):
        other = (place32 + n) % 32
        pl.semaphore_signal(
            barrier, inc=1, device_id=place(other // 8, x, (other // 2) % 4, other % 2), device_id_type=MESH
        )
    for n in range(1, 4):
        pl.semaphore_signal(barrier, inc=1, device_id=place(y, x + n, z, c), device_id_type=MESH)

    cols[...] = col_ref[...]
    rdeg[0] = row_ref[...]
    pl.semaphore_wait(barrier, 34)

    same = yh * 4
    lead = ((yh + c) % 2) * 4
    rest = 4 - lead
    x1, x2, xo = (x + 1 + 2 * c) % 4, (x + 3 + 2 * c) % 4, (x + 2) % 4
    dev1, dev2 = place(y, x1, z, c), place(y, x2, z, c)
    pair = place(y, x, z + 1 + 2 * c, 1 - c)
    step = ROWS // CHUNKS

    def piece(panel, k):
        return xs.at[panel, pl.ds(k * step, step)]

    def own_piece(k):
        return own.at[pl.ds(k * step, step)]

    chunks = range(CHUNKS)
    first = lead + x
    last = rest + x
    across = place(y + 2, x, z, c)
    to_y = jnp.where(c == 0, y, 3 - y)
    to_z = z + jnp.where(c == 0, q, 3 - 2 * yl)
    got = [
        send(own_piece(k), piece(same + x, k), s1_s.at[0, k], s1_r.at[0, k], place(to_y, x, to_z, c), q != 0)
        for k in chunks
    ]

    d1 = [
        send(cols, deg1.at[n - 1], d1_s.at[n - 1], d1_r.at[n - 1], place(y, x + n, z, c))
        for n in range(1, 4)
    ]
    rd = [
        send(rdeg.at[0], rdeg.at[n], rd_s.at[n - 1], rd_r.at[n - 1], (row, (q + n) % 4))
        for n in range(1, 4)
    ]

    @pl.when(q == 0)
    def _():
        xs[same + x] = own[...]

    loads[0].wait()

    @pl.when(q == 0)
    def _():
        eye = lax.broadcasted_iota(jnp.int32, (BLK, BLK), 0) == lax.broadcasted_iota(jnp.int32, (BLK, BLK), 1)
        eye = jnp.where(eye, 1.0, 0.0)
        for i in range(4):
            at = pl.ds(i * BLK, BLK), pl.ds(pl.multiple_of(first * ROWS + i * BLK, BLK), BLK)
            d[at] = (d[at].astype(F32) + eye).astype(BF16)

    def drain():
        for copy, when in sent:
            if when is None:
                copy.wait_send()
            else:
                pl.when(when)(copy.wait_send)
        sent.clear()

    def wait_when(copy, when):
        pl.when(when)(copy.wait_recv)

    by1, by2, got_rest = [[], []], [], []
    for k in chunks:
        wait_when(got[k], q != 0)
        src = piece(first, k)
        by2.append(send(src, src, x_s.at[2, k], x_r.at[2, k], dev2))
        by1[0].append(send(src, src, x_s.at[0, k], x_r.at[0, k], dev1))
        got_rest.append(send(src, src, s1_s.at[1, k], s1_r.at[1, k], across))

    for copy in d1:
        copy.wait_recv()
    deg2[0] = cols[...] + deg1[0] + deg1[1] + deg1[2]
    d2 = []
    for n in range(1, 8):
        o = (me8 + n) % 8
        o_q = o % 4
        to = place((o // 4) * 2 + o_q // 2, x, zp + o_q, o_q % 2)
        d2.append(send(deg2.at[0], deg2.at[n], d2_s.at[n - 1], d2_r.at[n - 1], to))

    onward, cross = [], [[], []]
    for k in chunks:
        by2[k].wait_recv()
        src = piece(lead + x1, k)
        onward.append(send(src, src, x_s.at[3, k], x_r.at[3, k], dev2))
    for k in chunks:
        by1[0][k].wait_recv()
        src = piece(lead + x2, k)
        cross[0].append(send(src, src, z_s.at[0, k], z_r.at[0, k], pair))
    for k in chunks:
        got_rest[k].wait_recv()
        src = piece(last, k)
        by1[1].append(send(src, src, x_s.at[1, k], x_r.at[1, k], dev1))

    for copy in rd:
        copy.wait_recv()
    by_rep = [rdeg[(q + 4 - s) % 4] for s in range(4)]
    row_scale = lax.rsqrt(1.0 + ((by_rep[0] + by_rep[1]) + (by_rep[2] + by_rep[3])))
    row_cols = jnp.concatenate([row_scale, row_scale], axis=0).T
    for i in range(4):
        rsc[i] = row_cols[:, i : i + 1]
    for copy in d2:
        copy.wait_recv()
    total = deg2[0]
    for n in range(1, 8):
        total = total + deg2[n]
    scales[...] = lax.rsqrt(1.0 + total)

    narrow = scales[...].astype(BF16)

    def scale_panel(p):
        for l in range(4 * p, 4 * p + 4):
            at = pl.ds(l * BLK, BLK)
            d[:, at] = d[:, at] * narrow[l : l + 1, :]

    for k in chunks:
        for p in range(8 * k // CHUNKS, 8 * (k + 1) // CHUNKS):
            scale_panel(p)
        onward[k].wait_recv()
        src = piece(lead + xo, k)
        cross[1].append(send(src, src, z_s.at[1, k], z_r.at[1, k], pair))

    def panel_cols(p):
        return pl.ds(pl.multiple_of(p * ROWS, ROWS), ROWS)

    def term(p):
        return jnp.dot(d[:, panel_cols(p)], xs[p], preferred_element_type=F32)

    lead4 = pl.ds(pl.multiple_of(lead * ROWS, ROWS), 4 * ROWS)
    acc = jnp.dot(d[:, lead4], xs[pl.ds(lead, 4)].reshape(4 * ROWS, FEAT), preferred_element_type=F32)
    acc = acc + term(last)
    for k in chunks:
        cross[0][k].wait_recv()
    acc = acc + term(rest + x1)
    for k in chunks:
        by1[1][k].wait_recv()
    acc = acc + term(rest + x2)
    for k in chunks:
        cross[1][k].wait_recv()
    acc = acc + term(rest + xo)
    hs[...] = acc.astype(BF16)
    loads[1].wait()

    half = ROWS // 2
    partner = place(y, x, z, 1 - c)
    chip = (row, (1 - yl) * 2 + c)

    def rows128(b):
        return pl.ds(pl.multiple_of(b * BLK, BLK), BLK)

    def project(b):
        part[rows128(b), :] = (
            jnp.dot(hs[rows128(b), :], w[...], preferred_element_type=F32) * 1.25
        ).astype(BF16)

    ec = [[], [], []]
    for b in range(2):
        project((1 - c) * 2 + b)
        ec[0].append(send(part.at[rows128((1 - c) * 2 + b)], e1.at[b], e_s.at[0, b], e_r.at[0, b], partner))
    project(c * 2)
    project(c * 2 + 1)
    for b in range(2):
        ec[0][b].wait_recv()
        e2s[b] = (part[rows128(c * 2 + b), :].astype(F32) + e1[b].astype(F32)).astype(BF16)
        ec[1].append(send(e2s.at[b], e2r.at[b], e_s.at[1, b], e_r.at[1, b], chip))
    e_sent = sent[-4:]
    del sent[-4:]
    drain()
    sent.extend(e_sent)
    hT[...] = acc.T.astype(BF16)
    loads[2].wait()

    def activate(i):
        at = rows128(i)
        r = rsc[i]
        pre = tot[at, :].astype(F32) * r
        s = 1.0 / (1.0 + jnp.exp(-pre))
        hid[at, :] = (pre * s).astype(BF16)
        grad = cot[at, :].astype(F32) * s * (1.0 + pre * (1.0 - s)) * r
        pushed[at, :] = grad.astype(BF16)
        pushT[:, at] = grad.T.astype(BF16)

    for b in range(2):
        ec[1][b].wait_recv()
        at = rows128(c * 2 + b)
        tot[at, :] = (e2s[b].astype(F32) + e2r[b].astype(F32)).astype(BF16)
        ec[2].append(send(tot.at[at], tot.at[at], e_s.at[2, b], e_r.at[2, b], partner))
    activate(c * 2)
    activate(c * 2 + 1)
    for b in range(2):
        ec[2][b].wait_recv()
        activate((1 - c) * 2 + b)

    g[...] = (jnp.dot(hT[...], pushed[...], preferred_element_type=F32) * 1.25).astype(BF16)
    place8 = y * 2 + c
    at32 = pl.ds(pl.multiple_of(place8 * 32, 32), 32)
    w1c = []
    for n in range(1, 8):
        o = (place8 + n) % 8
        src = g.at[pl.ds(pl.multiple_of(o * 32, 32), 32)]
        w1c.append(send(src, w1.at[n - 1], w1_s.at[n - 1], w1_r.at[n - 1], place(o // 2, x, z, o % 2)))

    def back(p):
        out = jnp.dot(pushT[...], d[:, panel_cols(p)], preferred_element_type=F32).astype(BF16)
        for j in range(4):
            tt[p, j] = out[:, j * BLK : (j + 1) * BLK]

    def add(*blocks):
        out = blocks[0].astype(F32)
        for block in blocks[1:]:
            out = out + block.astype(F32)
        return out.astype(BF16)

    blocks4 = range(4)
    zc, sidec, farc, nearc = [[], []], [[], []], [], []
    back(rest + xo)
    for j in blocks4:
        zc[0].append(send(tt.at[rest + xo, j], zb.at[0, j], zb_s.at[0, j], zb_r.at[0, j], pair))
    back(rest + x1)
    for j in blocks4:
        zc[1].append(send(tt.at[rest + x1, j], zb.at[1, j], zb_s.at[1, j], zb_r.at[1, j], pair))
    back(rest + x2)
    for j in blocks4:
        sidec[1].append(send(tt.at[rest + x2, j], bside.at[1, j], b_s.at[1, j], b_r.at[1, j], dev2))
    for copy in w1c:
        copy.wait_recv()
    w2[x] = add(g[at32, :], *[w1[n] for n in range(7)])
    w2c = [
        send(w2.at[x], w2.at[x], w2_s.at[n - 1], w2_r.at[n - 1], place(y, x + n, z, c)) for n in range(1, 4)
    ]

    back(last)
    back(lead + xo)
    for j in blocks4:
        zc[0][j].wait_recv()
        tt[lead + xo, j] = add(tt[lead + xo, j], zb[0, j])
        farc.append(send(tt.at[lead + xo, j], bfar.at[j], b_s.at[2, j], b_r.at[2, j], dev1))
    ypc = []
    for j in blocks4:
        sidec[1][j].wait_recv()
        u[1, j] = add(tt[last, j], bside[1, j])
        ypc.append(send(u.at[1, j], yp.at[j], yp_s.at[j], yp_r.at[j], across))

    for copy in w2c:
        copy.wait_recv()
    w3[z] = add(w2[0], w2[1], w2[2], w2[3])
    w3c = [
        send(w3.at[z], w3.at[z], w3_s.at[n - 1], w3_r.at[n - 1], place(y, x, z + n, c)) for n in range(1, 4)
    ]

    back(lead + x2)
    for j in blocks4:
        zc[1][j].wait_recv()
        tt[lead + x2, j] = add(tt[lead + x2, j], zb[1, j])
        sidec[0].append(send(tt.at[lead + x2, j], bside.at[0, j], b_s.at[0, j], b_r.at[0, j], dev2))

    back(lead + x1)
    for j in blocks4:
        farc[j].wait_recv()
        tt[lead + x1, j] = add(tt[lead + x1, j], bfar[j])
        nearc.append(send(tt.at[lead + x1, j], bnear.at[j], b_s.at[3, j], b_r.at[3, j], dev1))
    for copy in w3c:
        copy.wait_recv()
    g4[at32, :] = add(w3[0], w3[1], w3[2], w3[3])
    w4c = []
    for n in range(1, 8):
        o = (place8 + n) % 8
        src = g4.at[at32]
        w4c.append(send(src, src, w4_s.at[n - 1], w4_r.at[n - 1], place(o // 2, x, z, o % 2)))

    back(first)

    half_of = (yh + c) % 2
    for j in blocks4:
        sidec[0][j].wait_recv()
        nearc[j].wait_recv()
        ypc[j].wait_recv()
        u[0, j] = add(tt[first, j], bside[0, j], bnear[j], yp[j])
        to = place(2 * half_of + j // 2, x, zp, j % 2)
        send(u.at[0, j], fin.at[q], f_s.at[j], f_r.at[q], to, q != 0 if j == 0 else None)

    @pl.when(q == 0)
    def _():
        fin[0] = u[0, 0]

    f_sent = sent[-4:]
    del sent[-4:]
    drain()
    sent.extend(f_sent)

    for n in range(4):
        copy = remote(u.at[0, 0], fin.at[n], f_s.at[0], f_r.at[n], (row, q))
        if n == 0:
            wait_when(copy, q != 0)
        else:
            copy.wait_recv()
    proj = fin[0].astype(F32)
    for n in range(1, 4):
        proj = proj + fin[n].astype(F32)
    proj_ref[...] = proj.T.astype(BF16)
    for copy in w4c:
        copy.wait_recv()
    wg_ref[...] = g4[...]
    drain()


def layer(own, weight, d, col, row, cotangent):
    dma = pltpu.SemaphoreType.DMA
    vmem = pltpu.VMEM
    any_spec = pl.BlockSpec(memory_space=pl.ANY)
    vmem_spec = pl.BlockSpec(memory_space=pltpu.VMEM)
    return pl.pallas_call(
        layer_kernel,
        out_shape=[
            jax.ShapeDtypeStruct((ROWS, FEAT), BF16),
            jax.ShapeDtypeStruct((FEAT, FEAT), BF16),
            jax.ShapeDtypeStruct((BLK, FEAT), BF16),
            jax.ShapeDtypeStruct((FEAT, FEAT), BF16),
        ],
        in_specs=[vmem_spec, any_spec, any_spec, vmem_spec, vmem_spec, any_spec],
        out_specs=[vmem_spec] * 4,
        scratch_shapes=[
            vmem((ROWS, 32 * BLK), BF16),
            vmem((ROWS, FEAT), BF16),
            vmem((8, ROWS, FEAT), BF16),
            vmem((32, BLK), F32),
            vmem((32, BLK), F32),
            vmem((3, 32, BLK), F32),
            vmem((8, 32, BLK), F32),
            vmem((4, 4, BLK), F32),
            vmem((4, BLK, 1), F32),
            vmem((ROWS, FEAT), BF16),
            vmem((FEAT, ROWS), BF16),
            vmem((ROWS, FEAT), BF16),
            vmem((2, BLK, FEAT), BF16),
            vmem((2, BLK, FEAT), BF16),
            vmem((2, BLK, FEAT), BF16),
            vmem((ROWS, FEAT), BF16),
            vmem((ROWS, FEAT), BF16),
            vmem((FEAT, ROWS), BF16),
            vmem((8, 4, FEAT, BLK), BF16),
            vmem((2, 4, FEAT, BLK), BF16),
            vmem((4, FEAT, BLK), BF16),
            vmem((4, FEAT, BLK), BF16),
            vmem((2, 4, FEAT, BLK), BF16),
            vmem((2, 4, FEAT, BLK), BF16),
            vmem((4, FEAT, BLK), BF16),
            vmem((4, FEAT, BLK), BF16),
            vmem((FEAT, FEAT), BF16),
            vmem((7, 32, FEAT), BF16),
            vmem((4, 32, FEAT), BF16),
            vmem((4, 32, FEAT), BF16),
            vmem((FEAT, FEAT), BF16),
            dma((3,)),
            dma((2, CHUNKS)), dma((2, CHUNKS)),
            dma((4, CHUNKS)), dma((4, CHUNKS)),
            dma((2, CHUNKS)), dma((2, CHUNKS)),
            dma((3,)), dma((3,)), dma((7,)), dma((7,)), dma((3,)), dma((3,)),
            dma((3, 2)), dma((3, 2)),
            dma((2, 4)), dma((2, 4)), dma((4, 4)), dma((4, 4)),
            dma((4,)), dma((4,)), dma((4,)), dma((4,)),
            dma((7,)), dma((7,)), dma((3,)), dma((3,)), dma((3,)), dma((3,)),
            dma((7,)), dma((7,)),
        ],
        compiler_params=pltpu.CompilerParams(
            collective_id=0, has_side_effects=True, vmem_limit_bytes=24 << 20
        ),
        name="layer",
    )(own, weight, d, col, row, cotangent)


def finish_kernel(hid_ref, g_ref, proj_ref, w_ref, gate_ref, hid_out, wg_out, fg_out):
    hid_out[...] = hid_ref[...]
    wg_out[...] = g_ref[...].astype(F32)
    back_proj = (
        lax.dot_general(proj_ref[...], w_ref[...], (((1,), (1,)), ((), ())), preferred_element_type=F32) * 1.25
    )
    fg_out[...] = jnp.where(gate_ref[...] > 0.0, back_proj, 0.0).astype(BF16)


def finish(hid, g, proj, weight, gate):
    return pl.pallas_call(
        finish_kernel,
        out_shape=[
            jax.ShapeDtypeStruct((ROWS, FEAT), BF16),
            jax.ShapeDtypeStruct((FEAT, FEAT), F32),
            jax.ShapeDtypeStruct((BLK, FEAT), BF16),
        ],
        in_specs=[pl.BlockSpec(memory_space=pltpu.VMEM)] * 5,
        out_specs=[pl.BlockSpec(memory_space=pltpu.VMEM)] * 3,
        compiler_params=pltpu.CompilerParams(vmem_limit_bytes=4 << 20),
        name="finish",
    )(hid, g, proj, weight, gate)


def shards(features, weight, adj_tiles, block_cols, edge_keep, drop_key, cotangent):
    features, weight, adj_tiles, block_cols, edge_keep, drop_key, cotangent = (
        pltpu.with_memory_space_constraint(a, pltpu.HBM)
        for a in (features, weight, adj_tiles, block_cols, edge_keep, drop_key, cotangent)
    )
    own, gate, d, col, row = build(drop_key, block_cols, edge_keep, features, adj_tiles)
    hidden, grad, proj, kept_weight = layer(own, weight, d, col, row, cotangent)
    return finish(hidden, grad, proj, kept_weight, gate)


def solution(mesh):
    in_specs = (
        P("row", None),
        P(),
        P("row", "rep", None, None),
        P("row", "rep"),
        P("row", "rep"),
        P(),
        P("row", None),
    )
    out_specs = (P("row", None), P(), P(("row", "rep"), None))
    return jax.shard_map(shards, mesh=mesh, in_specs=in_specs, out_specs=out_specs, check_vma=False)
```

```python
import functools

import jax
import jax.numpy as jnp
from jax import lax
from jax.experimental import pallas as pl
from jax.experimental.pallas import tpu as pltpu
from jax.sharding import PartitionSpec as P

MESH = pl.DeviceIdType.MESH
BLK = 128
FEAT = 256
ROWS = 512
CHUNKS = 4
F32 = jnp.float32
BF16 = jnp.bfloat16


def keep_mask(node_ids, feat_ids, key0, key1):
    mixed = node_ids * 73856093 ^ feat_ids * 19349663 ^ key0 * 83492791 ^ key1
    mixed = mixed ^ lax.shift_right_logical(mixed, jnp.int32(13))
    mixed = mixed * 1274126177
    mixed = mixed ^ lax.shift_right_logical(mixed, jnp.int32(16))
    return mixed & 1023 < 819


def place(y, x, z, c):
    y, x, z = y % 4, x % 4, z % 4
    return ((y // 2) * 16 + x * 4 + z, (y % 2) * 2 + c)


def build_kernel(
    key_ref, blk_ref, keep_ref, feat_hbm, tiles_hbm, own_ref, gate_ref, d_ref, col_ref, row_ref, feat, tiles, sem
):
    loads = [pltpu.make_async_copy(tiles_hbm.at[i], tiles.at[i], sem.at[i]) for i in range(4)]
    loads.append(pltpu.make_async_copy(feat_hbm, feat, sem.at[4]))
    loads[4].start()
    for copy in loads[:4]:
        copy.start()
    col_ref[...] = jnp.zeros_like(col_ref)
    d_ref[...] = jnp.zeros_like(d_ref)

    first_node = lax.axis_index("row") * ROWS

    def kept(start):
        nodes = first_node + start + lax.broadcasted_iota(jnp.int32, (BLK, FEAT), 0)
        feats = lax.broadcasted_iota(jnp.int32, (BLK, FEAT), 1)
        return keep_mask(nodes, feats, key_ref[0], key_ref[1])

    gate_ref[...] = jnp.where(kept(lax.axis_index("rep") * BLK), 1.0, 0.0)
    loads[4].wait()
    for i in range(4):
        at = pl.ds(i * BLK, BLK)
        own_ref[at, :] = jnp.where(kept(i * BLK), feat[at, :].astype(F32), 0.0).astype(BF16)
    for i in range(4):
        loads[i].wait()
        rows = pl.ds(i * BLK, BLK)
        row_acc = jnp.zeros((BLK, BLK), F32)
        for k in range(16):
            col = blk_ref[i, k]
            slot = (col >> 4) * 4 + (col & 3)
            tile = tiles[i, k] * keep_ref[i, k].astype(BF16)
            at = pl.ds(pl.multiple_of(slot * BLK, BLK), BLK)
            d_ref[rows, at] = d_ref[rows, at] + tile
            wide = tile.astype(F32)
            col_ref[pl.ds(slot, 1), :] += jnp.sum(wide, axis=0, keepdims=True)
            row_acc = row_acc + wide
        row_ref[pl.ds(i, 1), :] = jnp.sum(row_acc.T, axis=0, keepdims=True)


def build(drop_key, cols, keep, features, tiles):
    smem, vmem = pl.BlockSpec(memory_space=pltpu.SMEM), pl.BlockSpec(memory_space=pltpu.VMEM)
    any_spec = pl.BlockSpec(memory_space=pl.ANY)
    return pl.pallas_call(
        build_kernel,
        in_specs=[smem, smem, smem, any_spec, any_spec],
        out_specs=[vmem] * 5,
        out_shape=[
            jax.ShapeDtypeStruct((ROWS, FEAT), BF16),
            jax.ShapeDtypeStruct((BLK, FEAT), F32),
            jax.ShapeDtypeStruct((ROWS, 32 * BLK), BF16),
            jax.ShapeDtypeStruct((32, BLK), F32),
            jax.ShapeDtypeStruct((4, BLK), F32),
        ],
        scratch_shapes=[
            pltpu.VMEM((ROWS, FEAT), BF16),
            pltpu.VMEM((4, 16, BLK, BLK), BF16),
            pltpu.SemaphoreType.DMA((5,)),
        ],
        compiler_params=pltpu.CompilerParams(vmem_limit_bytes=12 << 20),
        name="build",
    )(drop_key, cols, keep, features, tiles)


def layer_kernel(
    own, w_hbm, d_hbm, col_ref, row_ref, cot_hbm,
    hid, wg_ref, proj_ref, w,
    d, cot, xs, cols, scales, deg1, deg2, rdeg, rsc, hs, hT, part, e1, e2s, e2r, tot,
    pushed, pushT, tt, zb, bfar, bnear, bside, u, yp, fin, g, w1, w2, w3, g4,
    in_sem, s1_s, s1_r, x_s, x_r, z_s, z_r, d1_s, d1_r, d2_s, d2_r, rd_s, rd_r,
    e_s, e_r, zb_s, zb_r, b_s, b_r, yp_s, yp_r, f_s, f_r,
    w1_s, w1_r, w2_s, w2_r, w3_s, w3_r, w4_s, w4_r,
):
    row = lax.axis_index("row")
    q = lax.axis_index("rep")
    y = (row // 16) * 2 + q // 2
    x = (row // 4) % 4
    z = row % 4
    c = q % 2
    yh = row // 16
    yl = q // 2
    zp = z + 4 - q
    me8 = yh * 4 + q
    sent = []

    def remote(src, dst, ssem, rsem, to):
        return pltpu.make_async_remote_copy(
            src_ref=src, dst_ref=dst, send_sem=ssem, recv_sem=rsem, device_id=to, device_id_type=MESH
        )

    def send(src, dst, ssem, rsem, to, when=None):
        copy = remote(src, dst, ssem, rsem, to)
        if when is None:
            copy.start()
        else:
            pl.when(when)(copy.start)
        sent.append((copy, when))
        return copy

    loads = [
        pltpu.make_async_copy(src, dst, in_sem.at[n])
        for n, (src, dst) in enumerate(((d_hbm, d), (w_hbm, w), (cot_hbm, cot)))
    ]
    for copy in loads:
        copy.start()

    barrier = pltpu.get_barrier_semaphore()
    place32 = y * 8 + z * 2 + c
    for n in range(1, 32):
        other = (place32 + n) % 32
        pl.semaphore_signal(
            barrier, inc=1, device_id=place(other // 8, x, (other // 2) % 4, other % 2), device_id_type=MESH
        )
    for n in range(1, 4):
        pl.semaphore_signal(barrier, inc=1, device_id=place(y, x + n, z, c), device_id_type=MESH)

    cols[...] = col_ref[...]
    rdeg[0] = row_ref[...]
    pl.semaphore_wait(barrier, 34)

    same = yh * 4
    lead = ((yh + c) % 2) * 4
    rest = 4 - lead
    x1, x2, xo = (x + 1 + 2 * c) % 4, (x + 3 + 2 * c) % 4, (x + 2) % 4
    dev1, dev2 = place(y, x1, z, c), place(y, x2, z, c)
    pair = place(y, x, z + 1 + 2 * c, 1 - c)
    step = ROWS // CHUNKS

    def piece(panel, k):
        return xs.at[panel, pl.ds(k * step, step)]

    def own_piece(k):
        return own.at[pl.ds(k * step, step)]

    chunks = range(CHUNKS)
    first = lead + x
    last = rest + x
    across = place(y + 2, x, z, c)
    to_y = jnp.where(c == 0, y, 3 - y)
    to_z = z + jnp.where(c == 0, q, 3 - 2 * yl)
    got = [
        send(own_piece(k), piece(same + x, k), s1_s.at[0, k], s1_r.at[0, k], place(to_y, x, to_z, c), q != 0)
        for k in chunks
    ]

    d1 = [
        send(cols, deg1.at[n - 1], d1_s.at[n - 1], d1_r.at[n - 1], place(y, x + n, z, c))
        for n in range(1, 4)
    ]
    rd = [
        send(rdeg.at[0], rdeg.at[n], rd_s.at[n - 1], rd_r.at[n - 1], (row, (q + n) % 4))
        for n in range(1, 4)
    ]

    @pl.when(q == 0)
    def _():
        xs[same + x] = own[...]

    loads[0].wait()

    @pl.when(q == 0)
    def _():
        eye = lax.broadcasted_iota(jnp.int32, (BLK, BLK), 0) == lax.broadcasted_iota(jnp.int32, (BLK, BLK), 1)
        eye = jnp.where(eye, 1.0, 0.0)
        for i in range(4):
            at = pl.ds(i * BLK, BLK), pl.ds(pl.multiple_of(first * ROWS + i * BLK, BLK), BLK)
            d[at] = (d[at].astype(F32) + eye).astype(BF16)

    def drain():
        for copy, when in sent:
            if when is None:
                copy.wait_send()
            else:
                pl.when(when)(copy.wait_send)
        sent.clear()

    def wait_when(copy, when):
        pl.when(when)(copy.wait_recv)

    by1, by2, got_rest = [[], []], [], []
    for k in chunks:
        wait_when(got[k], q != 0)
        src = piece(first, k)
        by2.append(send(src, src, x_s.at[2, k], x_r.at[2, k], dev2))
        by1[0].append(send(src, src, x_s.at[0, k], x_r.at[0, k], dev1))
        got_rest.append(send(src, src, s1_s.at[1, k], s1_r.at[1, k], across))

    for copy in d1:
        copy.wait_recv()
    deg2[0] = cols[...] + deg1[0] + deg1[1] + deg1[2]
    d2 = []
    for n in range(1, 8):
        o = (me8 + n) % 8
        o_q = o % 4
        to = place((o // 4) * 2 + o_q // 2, x, zp + o_q, o_q % 2)
        d2.append(send(deg2.at[0], deg2.at[n], d2_s.at[n - 1], d2_r.at[n - 1], to))

    onward, cross = [], [[], []]
    for k in chunks:
        by2[k].wait_recv()
        src = piece(lead + x1, k)
        onward.append(send(src, src, x_s.at[3, k], x_r.at[3, k], dev2))
    for k in chunks:
        by1[0][k].wait_recv()
        src = piece(lead + x2, k)
        cross[0].append(send(src, src, z_s.at[0, k], z_r.at[0, k], pair))
    for k in chunks:
        got_rest[k].wait_recv()
        src = piece(last, k)
        by1[1].append(send(src, src, x_s.at[1, k], x_r.at[1, k], dev1))

    for copy in rd:
        copy.wait_recv()
    by_rep = [rdeg[(q + 4 - s) % 4] for s in range(4)]
    row_scale = lax.rsqrt(1.0 + ((by_rep[0] + by_rep[1]) + (by_rep[2] + by_rep[3])))
    row_cols = jnp.concatenate([row_scale, row_scale], axis=0).T
    for i in range(4):
        rsc[i] = row_cols[:, i : i + 1]
    for copy in d2:
        copy.wait_recv()
    total = deg2[0]
    for n in range(1, 8):
        total = total + deg2[n]
    scales[...] = lax.rsqrt(1.0 + total)

    narrow = scales[...].astype(BF16)

    def scale_panel(p):
        for l in range(4 * p, 4 * p + 4):
            at = pl.ds(l * BLK, BLK)
            d[:, at] = d[:, at] * narrow[l : l + 1, :]

    for k in chunks:
        for p in range(8 * k // CHUNKS, 8 * (k + 1) // CHUNKS):
            scale_panel(p)
        onward[k].wait_recv()
        src = piece(lead + xo, k)
        cross[1].append(send(src, src, z_s.at[1, k], z_r.at[1, k], pair))

    def panel_cols(p):
        return pl.ds(pl.multiple_of(p * ROWS, ROWS), ROWS)

    def term(p):
        return jnp.dot(d[:, panel_cols(p)], xs[p], preferred_element_type=F32)

    lead4 = pl.ds(pl.multiple_of(lead * ROWS, ROWS), 4 * ROWS)
    acc = jnp.dot(d[:, lead4], xs[pl.ds(lead, 4)].reshape(4 * ROWS, FEAT), preferred_element_type=F32)
    acc = acc + term(last)
    for k in chunks:
        cross[0][k].wait_recv()
    acc = acc + term(rest + x1)
    for k in chunks:
        by1[1][k].wait_recv()
    acc = acc + term(rest + x2)
    for k in chunks:
        cross[1][k].wait_recv()
    acc = acc + term(rest + xo)
    hs[...] = acc.astype(BF16)
    loads[1].wait()

    half = ROWS // 2
    partner = place(y, x, z, 1 - c)
    chip = (row, (1 - yl) * 2 + c)

    def rows128(b):
        return pl.ds(pl.multiple_of(b * BLK, BLK), BLK)

    def project(b):
        part[rows128(b), :] = (
            jnp.dot(hs[rows128(b), :], w[...], preferred_element_type=F32) * 1.25
        ).astype(BF16)

    ec = [[], [], []]
    for b in range(2):
        project((1 - c) * 2 + b)
        ec[0].append(send(part.at[rows128((1 - c) * 2 + b)], e1.at[b], e_s.at[0, b], e_r.at[0, b], partner))
    project(c * 2)
    project(c * 2 + 1)
    for b in range(2):
        ec[0][b].wait_recv()
        e2s[b] = (part[rows128(c * 2 + b), :].astype(F32) + e1[b].astype(F32)).astype(BF16)
        ec[1].append(send(e2s.at[b], e2r.at[b], e_s.at[1, b], e_r.at[1, b], chip))
    e_sent = sent[-4:]
    del sent[-4:]
    drain()
    sent.extend(e_sent)
    hT[...] = acc.T.astype(BF16)
    loads[2].wait()

    def activate(i):
        at = rows128(i)
        r = rsc[i]
        pre = tot[at, :].astype(F32) * r
        s = 1.0 / (1.0 + jnp.exp(-pre))
        hid[at, :] = (pre * s).astype(BF16)
        grad = cot[at, :].astype(F32) * s * (1.0 + pre * (1.0 - s)) * r
        pushed[at, :] = grad.astype(BF16)
        pushT[:, at] = grad.T.astype(BF16)

    for b in range(2):
        ec[1][b].wait_recv()
        at = rows128(c * 2 + b)
        tot[at, :] = (e2s[b].astype(F32) + e2r[b].astype(F32)).astype(BF16)
        ec[2].append(send(tot.at[at], tot.at[at], e_s.at[2, b], e_r.at[2, b], partner))
    activate(c * 2)
    activate(c * 2 + 1)
    for b in range(2):
        ec[2][b].wait_recv()
        activate((1 - c) * 2 + b)

    def back(p):
        out = jnp.dot(pushT[...], d[:, panel_cols(p)], preferred_element_type=F32).astype(BF16)
        for j in range(4):
            tt[p, j] = out[:, j * BLK : (j + 1) * BLK]

    def add(*blocks):
        out = blocks[0].astype(F32)
        for block in blocks[1:]:
            out = out + block.astype(F32)
        return out.astype(BF16)

    blocks4 = range(4)
    zc, sidec, farc, nearc = [[], []], [[], []], [], []
    back(rest + xo)
    for j in blocks4:
        zc[0].append(send(tt.at[rest + xo, j], zb.at[0, j], zb_s.at[0, j], zb_r.at[0, j], pair))
    g[...] = (jnp.dot(hT[...], pushed[...], preferred_element_type=F32) * 1.25).astype(BF16)
    place8 = y * 2 + c
    at32 = pl.ds(pl.multiple_of(place8 * 32, 32), 32)
    w1c = []
    for n in range(1, 8):
        o = (place8 + n) % 8
        src = g.at[pl.ds(pl.multiple_of(o * 32, 32), 32)]
        w1c.append(send(src, w1.at[n - 1], w1_s.at[n - 1], w1_r.at[n - 1], place(o // 2, x, z, o % 2)))

    back(rest + x1)
    for j in blocks4:
        zc[1].append(send(tt.at[rest + x1, j], zb.at[1, j], zb_s.at[1, j], zb_r.at[1, j], pair))
    back(rest + x2)
    for j in blocks4:
        sidec[1].append(send(tt.at[rest + x2, j], bside.at[1, j], b_s.at[1, j], b_r.at[1, j], dev2))
    for copy in w1c:
        copy.wait_recv()
    w2[x] = add(g[at32, :], *[w1[n] for n in range(7)])
    w2c = [
        send(w2.at[x], w2.at[x], w2_s.at[n - 1], w2_r.at[n - 1], place(y, x + n, z, c)) for n in range(1, 4)
    ]

    back(last)
    back(lead + xo)
    for j in blocks4:
        zc[0][j].wait_recv()
        tt[lead + xo, j] = add(tt[lead + xo, j], zb[0, j])
        farc.append(send(tt.at[lead + xo, j], bfar.at[j], b_s.at[2, j], b_r.at[2, j], dev1))
    ypc = []
    for j in blocks4:
        sidec[1][j].wait_recv()
        u[1, j] = add(tt[last, j], bside[1, j])
        ypc.append(send(u.at[1, j], yp.at[j], yp_s.at[j], yp_r.at[j], across))

    for copy in w2c:
        copy.wait_recv()
    w3[z] = add(w2[0], w2[1], w2[2], w2[3])
    w3c = [
        send(w3.at[z], w3.at[z], w3_s.at[n - 1], w3_r.at[n - 1], place(y, x, z + n, c)) for n in range(1, 4)
    ]

    back(lead + x2)
    for j in blocks4:
        zc[1][j].wait_recv()
        tt[lead + x2, j] = add(tt[lead + x2, j], zb[1, j])
        sidec[0].append(send(tt.at[lead + x2, j], bside.at[0, j], b_s.at[0, j], b_r.at[0, j], dev2))

    back(lead + x1)
    for j in blocks4:
        farc[j].wait_recv()
        tt[lead + x1, j] = add(tt[lead + x1, j], bfar[j])
        nearc.append(send(tt.at[lead + x1, j], bnear.at[j], b_s.at[3, j], b_r.at[3, j], dev1))
    for copy in w3c:
        copy.wait_recv()
    g4[at32, :] = add(w3[0], w3[1], w3[2], w3[3])
    w4c = []
    for n in range(1, 8):
        o = (place8 + n) % 8
        src = g4.at[at32]
        w4c.append(send(src, src, w4_s.at[n - 1], w4_r.at[n - 1], place(o // 2, x, z, o % 2)))

    back(first)

    half_of = (yh + c) % 2
    for j in blocks4:
        sidec[0][j].wait_recv()
        nearc[j].wait_recv()
        ypc[j].wait_recv()
        u[0, j] = add(tt[first, j], bside[0, j], bnear[j], yp[j])
        to = place(2 * half_of + j // 2, x, zp, j % 2)
        send(u.at[0, j], fin.at[q], f_s.at[j], f_r.at[q], to, q != 0 if j == 0 else None)

    @pl.when(q == 0)
    def _():
        fin[0] = u[0, 0]

    f_sent = sent[-4:]
    del sent[-4:]
    drain()
    sent.extend(f_sent)

    for n in range(4):
        copy = remote(u.at[0, 0], fin.at[n], f_s.at[0], f_r.at[n], (row, q))
        if n == 0:
            wait_when(copy, q != 0)
        else:
            copy.wait_recv()
    proj = fin[0].astype(F32)
    for n in range(1, 4):
        proj = proj + fin[n].astype(F32)
    proj_ref[...] = proj.T.astype(BF16)
    for copy in w4c:
        copy.wait_recv()
    wg_ref[...] = g4[...]
    drain()


def layer(own, weight, d, col, row, cotangent):
    dma = pltpu.SemaphoreType.DMA
    vmem = pltpu.VMEM
    any_spec = pl.BlockSpec(memory_space=pl.ANY)
    vmem_spec = pl.BlockSpec(memory_space=pltpu.VMEM)
    return pl.pallas_call(
        layer_kernel,
        out_shape=[
            jax.ShapeDtypeStruct((ROWS, FEAT), BF16),
            jax.ShapeDtypeStruct((FEAT, FEAT), BF16),
            jax.ShapeDtypeStruct((BLK, FEAT), BF16),
            jax.ShapeDtypeStruct((FEAT, FEAT), BF16),
        ],
        in_specs=[vmem_spec, any_spec, any_spec, vmem_spec, vmem_spec, any_spec],
        out_specs=[vmem_spec] * 4,
        scratch_shapes=[
            vmem((ROWS, 32 * BLK), BF16),
            vmem((ROWS, FEAT), BF16),
            vmem((8, ROWS, FEAT), BF16),
            vmem((32, BLK), F32),
            vmem((32, BLK), F32),
            vmem((3, 32, BLK), F32),
            vmem((8, 32, BLK), F32),
            vmem((4, 4, BLK), F32),
            vmem((4, BLK, 1), F32),
            vmem((ROWS, FEAT), BF16),
            vmem((FEAT, ROWS), BF16),
            vmem((ROWS, FEAT), BF16),
            vmem((2, BLK, FEAT), BF16),
            vmem((2, BLK, FEAT), BF16),
            vmem((2, BLK, FEAT), BF16),
            vmem((ROWS, FEAT), BF16),
            vmem((ROWS, FEAT), BF16),
            vmem((FEAT, ROWS), BF16),
            vmem((8, 4, FEAT, BLK), BF16),
            vmem((2, 4, FEAT, BLK), BF16),
            vmem((4, FEAT, BLK), BF16),
            vmem((4, FEAT, BLK), BF16),
            vmem((2, 4, FEAT, BLK), BF16),
            vmem((2, 4, FEAT, BLK), BF16),
            vmem((4, FEAT, BLK), BF16),
            vmem((4, FEAT, BLK), BF16),
            vmem((FEAT, FEAT), BF16),
            vmem((7, 32, FEAT), BF16),
            vmem((4, 32, FEAT), BF16),
            vmem((4, 32, FEAT), BF16),
            vmem((FEAT, FEAT), BF16),
            dma((3,)),
            dma((2, CHUNKS)), dma((2, CHUNKS)),
            dma((4, CHUNKS)), dma((4, CHUNKS)),
            dma((2, CHUNKS)), dma((2, CHUNKS)),
            dma((3,)), dma((3,)), dma((7,)), dma((7,)), dma((3,)), dma((3,)),
            dma((3, 2)), dma((3, 2)),
            dma((2, 4)), dma((2, 4)), dma((4, 4)), dma((4, 4)),
            dma((4,)), dma((4,)), dma((4,)), dma((4,)),
            dma((7,)), dma((7,)), dma((3,)), dma((3,)), dma((3,)), dma((3,)),
            dma((7,)), dma((7,)),
        ],
        compiler_params=pltpu.CompilerParams(
            collective_id=0, has_side_effects=True, vmem_limit_bytes=24 << 20
        ),
        name="layer",
    )(own, weight, d, col, row, cotangent)


def finish_kernel(hid_ref, g_ref, proj_ref, w_ref, gate_ref, hid_out, wg_out, fg_out):
    hid_out[...] = hid_ref[...]
    wg_out[...] = g_ref[...].astype(F32)
    back_proj = (
        lax.dot_general(proj_ref[...], w_ref[...], (((1,), (1,)), ((), ())), preferred_element_type=F32) * 1.25
    )
    fg_out[...] = jnp.where(gate_ref[...] > 0.0, back_proj, 0.0).astype(BF16)


def finish(hid, g, proj, weight, gate):
    return pl.pallas_call(
        finish_kernel,
        out_shape=[
            jax.ShapeDtypeStruct((ROWS, FEAT), BF16),
            jax.ShapeDtypeStruct((FEAT, FEAT), F32),
            jax.ShapeDtypeStruct((BLK, FEAT), BF16),
        ],
        in_specs=[pl.BlockSpec(memory_space=pltpu.VMEM)] * 5,
        out_specs=[pl.BlockSpec(memory_space=pltpu.VMEM)] * 3,
        compiler_params=pltpu.CompilerParams(vmem_limit_bytes=4 << 20),
        name="finish",
    )(hid, g, proj, weight, gate)


def shards(features, weight, adj_tiles, block_cols, edge_keep, drop_key, cotangent):
    features, weight, adj_tiles, block_cols, edge_keep, drop_key, cotangent = (
        pltpu.with_memory_space_constraint(a, pltpu.HBM)
        for a in (features, weight, adj_tiles, block_cols, edge_keep, drop_key, cotangent)
    )
    own, gate, d, col, row = build(drop_key, block_cols, edge_keep, features, adj_tiles)
    hidden, grad, proj, kept_weight = layer(own, weight, d, col, row, cotangent)
    return finish(hidden, grad, proj, kept_weight, gate)


def solution(mesh):
    in_specs = (
        P("row", None),
        P(),
        P("row", "rep", None, None),
        P("row", "rep"),
        P("row", "rep"),
        P(),
        P("row", None),
    )
    out_specs = (P("row", None), P(), P(("row", "rep"), None))
    return jax.shard_map(shards, mesh=mesh, in_specs=in_specs, out_specs=out_specs, check_vma=False)
```
